256 devices in a mesh: azim: 16 (over x_lo, z), cross: 8 (over x_hi, y), role: 2 (over core).
Axes of the slice: x: 4 (x_hi: 2, x_lo: 2; x = x_hi * 2 + x_lo), y: 4, z: 8, core: 2. Of those that a mesh axis runs over, the one named last changes fastest.
Arguments:
- checkpoint: float32 [8, 16, 32, 2048], P(None, ('cross', 'role'), None, 'azim'), may hold values from -1.2 to 8.1, as said below
- primary_arrhenius_exponent: float32 [16, 32, 2048], P(('cross', 'role'), None, 'azim'), may hold values from 0 to 2.3
- cell_types: int32 [16, 32, 2048], P(('cross', 'role'), None, 'azim'), may hold values from 0 to 2
- final_adjoint: float32 [8, 16, 32, 2048], P(None, None, ('cross', 'role'), 'azim'), may hold values from -6 to 6
Outputs:
- adjoint_start: float32 [8, 16, 32, 2048], P(None, None, ('cross', 'role'), 'azim')
- rate_gradient: float32 [16, 32, 2048], P(None, ('cross', 'role'), 'azim')
The draws below stay inside these ranges and needn't reach their ends.
Inputs may be any that keep to these rules, and one draw needn't show every extreme that they name: `checkpoint`: density lies between 0.7 and 1.4 and pressure between 0.35 and 2 in every cell; fuel, radical and product densities are nonnegative and at most the density.
All inputs are finite; a program needn't handle non-finite values.
Results may differ from the reference program's by a relative error of at most 0.0003.
Values sent between devices are 32-bit elements; how exact they have to be, the bound alone decides.
No kernel may reach another device: no remote copies, remote signals or barrier semaphores. Data moves between devices by JAX's collectives and lax.ppermute only.
A program may use at most 64 MiB of HBM per device.

```python
import math
import jax
import jax.numpy as jnp
from jax import lax

CA = 128
FIELDS = 8
NZ = 16
NR = 32
NA = 2048
N_AZIM = 16


HEAT_RATIO = 1.3


def draw_checkpoint(key, part):
    grid_shape = (NZ, NR, NA)
    subkeys = jax.random.split(jax.random.fold_in(key, 7), 8)
    volumetric_weight = jax.random.uniform(subkeys[0], grid_shape, jnp.float32, 0.7, 1.4)
    speeds = [jnp.clip(0.3 * jax.random.normal(subkeys[i], grid_shape, jnp.float32), -0.8, 0.8) for i in (1, 2, 3)]
    thermodynamic_stress = jnp.exp(jax.random.uniform(subkeys[4], grid_shape, jnp.float32, math.log(0.5), math.log(2.0)))
    fractions = [jax.random.uniform(subkeys[i], grid_shape, jnp.float32, 0.0, 1.0) for i in (5, 6, 7)]
    kinetic = 0.5 * volumetric_weight * (speeds[0] * speeds[0] + speeds[1] * speeds[1] + speeds[2] * speeds[2])
    energy = thermodynamic_stress / (HEAT_RATIO - 1.0) + kinetic
    return jnp.stack([volumetric_weight, volumetric_weight * speeds[0], volumetric_weight * speeds[1], volumetric_weight * speeds[2], energy, volumetric_weight * fractions[0], volumetric_weight * fractions[1], volumetric_weight * fractions[2]]).astype(jnp.float32)


def touch_ends(values, own_key, smallest, largest):
    longest = values.shape.index(max(values.shape))
    spots = []
    for shift in (0, 1):
        where = [jax.random.randint(jax.random.fold_in(own_key, axis), (), 0, length) for axis, length in enumerate(values.shape)]
        where[longest] = (where[longest] + shift) % values.shape[longest]
        spots.append(tuple(where))
    return values.at[spots[0]].set(smallest).at[spots[1]].set(largest)


def block_scale(own_key, shape, cuts, least, largest):
    gain, own = 1.0, jax.random.fold_in(own_key, 6)
    for axis_at, shards_of in cuts:
        draws = jnp.exp(jax.random.uniform(jax.random.fold_in(own, axis_at), (shards_of,), jnp.float32, least / len(cuts), largest / len(cuts)))
        gain = gain * jnp.repeat(draws, shape[axis_at] // shards_of).reshape([-1 if axis == axis_at else 1 for axis in range(len(shape))])
    return gain


def bell_draw(stream_key, extent, width, most, cuts=(), kind=jnp.bfloat16):
    values = jax.random.normal(stream_key, extent, jnp.float32) * width
    if len(cuts) > 0:
        values = block_scale(stream_key, extent, cuts, -0.22, 0.18) * values
    return jnp.clip(values, min=-most, max=most).astype(kind)


def setup_inputs(seed: int = 0) -> dict:
    keys = jax.random.split(jax.random.key(seed), 5)
    return {
        "checkpoint": draw_checkpoint(jax.random.fold_in(keys[4], 71), 0),
        "primary_arrhenius_exponent": jnp.clip(2.3 * jax.random.uniform(keys[1], (NZ, NR, NA), jnp.float32) ** block_scale(keys[1], (NZ, NR, NA), ((0, 16), (2, 16)), -0.2, 0.2), 0.0, 2.3),
        "cell_types": touch_ends(jax.random.randint(keys[2], (NZ, NR, NA), 0, 3), jax.random.fold_in(keys[2], 1), 0, 2).astype(jnp.int32),
        "final_adjoint": bell_draw(keys[3], (FIELDS, NZ, NR, NA), 1.0, 6.0, ((2, 16), (3, 16)), jnp.float32),
    }


HEAT_RATIO = 1.3
WAVE_SPEED = 4.0
TIME_STEP = 0.06
PRIMARY_BARRIER = 1.0
SECONDARY_ENERGY = 1.5
SECONDARY_SCALE = 2.0
HEAT_FIRST = 3.0
HEAT_SECOND = 2.0
INJECT_RELAX = 2.0
SPONGE_RELAX = 1.0
FRESH_STATE = (1.0, 0.8, 0.0, 0.0, 1.0 / (HEAT_RATIO - 1.0) + 0.32, 1.0, 0.0, 0.0)
DAMPED_ROWS = (0.0, 1.0, 1.0, 1.0, 0.0, 0.0, 0.0, 0.0)

def cell_flux(fields, which_axis):
    volumetric_weight = fields[0]
    velocity = fields[which_axis] / volumetric_weight
    thermodynamic_stress = (HEAT_RATIO - 1.0) * (fields[4] - 0.5 * (fields[1] * fields[1] + fields[2] * fields[2] + fields[3] * fields[3]) / volumetric_weight)
    carried = fields * velocity[None]
    carried = carried.at[which_axis].add(thermodynamic_stress)
    carried = carried.at[4].add(thermodynamic_stress * velocity)
    return carried

def flux_difference(fields, which_axis):
    count = fields.shape[which_axis]
    values = cell_flux(fields, which_axis)
    lower_values = lax.slice_in_dim(values, 0, count - 1, axis=which_axis)
    upper_values = lax.slice_in_dim(values, 1, count, axis=which_axis)
    lower_fields = lax.slice_in_dim(fields, 0, count - 1, axis=which_axis)
    upper_fields = lax.slice_in_dim(fields, 1, count, axis=which_axis)
    face_flux = 0.5 * (lower_values + upper_values) - 0.5 * WAVE_SPEED * (upper_fields - lower_fields)
    return lax.slice_in_dim(face_flux, 1, count - 1, axis=which_axis) - lax.slice_in_dim(face_flux, 0, count - 2, axis=which_axis)

def section_update(padded, primary_arrhenius_exponent, cell_kinds):
    divergence = flux_difference(padded[:, :, 1:-1, 1:-1], 1)
    divergence = divergence + flux_difference(padded[:, 1:-1, :, 1:-1], 2)
    divergence = divergence + flux_difference(padded[:, 1:-1, 1:-1, :], 3)
    middle_volumes = padded[:, 1:-1, 1:-1, 1:-1]
    volumetric_weight = middle_volumes[0]
    thermodynamic_stress = (HEAT_RATIO - 1.0) * (middle_volumes[4] - 0.5 * (middle_volumes[1] * middle_volumes[1] + middle_volumes[2] * middle_volumes[2] + middle_volumes[3] * middle_volumes[3]) / volumetric_weight)
    thermal_kelvin = thermodynamic_stress / volumetric_weight
    primary_reaction_speed = jnp.exp(primary_arrhenius_exponent - PRIMARY_BARRIER / thermal_kelvin) * middle_volumes[5]
    secondary_reaction_speed = SECONDARY_SCALE * jnp.exp(-SECONDARY_ENERGY / thermal_kelvin) * middle_volumes[6]
    nothing = jnp.zeros_like(primary_reaction_speed)
    reaction = jnp.stack([nothing, nothing, nothing, nothing, HEAT_FIRST * primary_reaction_speed + HEAT_SECOND * secondary_reaction_speed, -primary_reaction_speed, primary_reaction_speed - secondary_reaction_speed, secondary_reaction_speed])
    inject = jnp.where(cell_kinds == 1.0, 1.0, 0.0).astype(middle_volumes.dtype)
    sponge = jnp.where(cell_kinds == 2.0, 1.0, 0.0).astype(middle_volumes.dtype)
    fresh = jnp.array(FRESH_STATE, dtype=middle_volumes.dtype).reshape(8, 1, 1, 1)
    damped = jnp.array(DAMPED_ROWS, dtype=middle_volumes.dtype).reshape(8, 1, 1, 1)
    source = reaction + INJECT_RELAX * inject[None] * (fresh - middle_volumes) - SPONGE_RELAX * sponge[None] * damped * middle_volumes
    return middle_volumes + TIME_STEP * (source - divergence)

def wrap_azimuth(fields):
    return jnp.concatenate([fields[..., -1:], fields, fields[..., :1]], axis=-1)

def pad_ends(window):
    return jnp.pad(window, ((0, 0), (1, 1), (1, 1), (0, 0)), mode='edge')

def blocks_to_grid(stacked):
    moved = jnp.moveaxis(stacked, 0, -2)
    return moved.reshape(moved.shape[:-2] + (moved.shape[-2] * moved.shape[-1],))

def apply_section(fields, primary_arrhenius_exponent, cell_kinds):
    wrapped = wrap_azimuth(fields)

    def one_block(block_index):
        start = block_index * CA
        window = lax.dynamic_slice_in_dim(wrapped, start, CA + 2, axis=3)
        rate_block = lax.dynamic_slice_in_dim(primary_arrhenius_exponent, start, CA, axis=2)
        kind_block = lax.dynamic_slice_in_dim(cell_kinds, start, CA, axis=2)
        return section_update(pad_ends(window), rate_block, kind_block)
    return blocks_to_grid(lax.map(one_block, jnp.arange(N_AZIM, dtype=jnp.int32)))

def adjoint_section(fields, cotangent, primary_arrhenius_exponent, cell_kinds):
    wrapped = wrap_azimuth(fields)

    def one_block(block_index):
        start = block_index * CA
        window = lax.dynamic_slice_in_dim(wrapped, start, CA + 2, axis=3)
        rate_block = lax.dynamic_slice_in_dim(primary_arrhenius_exponent, start, CA, axis=2)
        kind_block = lax.dynamic_slice_in_dim(cell_kinds, start, CA, axis=2)
        cot_block = lax.dynamic_slice_in_dim(cotangent, start, CA, axis=3)

        def local(window_in, rate_in):
            return section_update(pad_ends(window_in), rate_in, kind_block)
        unused, pullback = jax.vjp(local, window, rate_block)
        return pullback(cot_block)
    window_cot, rate_cot = lax.map(one_block, jnp.arange(N_AZIM, dtype=jnp.int32))
    interior = window_cot[..., 1:-1]
    left_ghost = window_cot[..., 0]
    right_ghost = window_cot[..., -1]
    interior = interior.at[..., -1].add(jnp.roll(left_ghost, -1, axis=0))
    interior = interior.at[..., 0].add(jnp.roll(right_ghost, 1, axis=0))
    return (blocks_to_grid(interior), blocks_to_grid(rate_cot))

def reference(checkpoint, primary_arrhenius_exponent, cell_types, final_adjoint):
    cell_kinds = cell_types.astype(jnp.float32)
    state_zero = checkpoint
    state_one = apply_section(state_zero, primary_arrhenius_exponent, cell_kinds)
    state_two = 0.5 * state_zero + 0.5 * apply_section(state_one, primary_arrhenius_exponent, cell_kinds)
    state_three = apply_section(state_two, primary_arrhenius_exponent, cell_kinds)
    cot_three, grad_three = adjoint_section(state_three, 0.5 * final_adjoint, primary_arrhenius_exponent, cell_kinds)
    cot_back, grad_two = adjoint_section(state_two, cot_three, primary_arrhenius_exponent, cell_kinds)
    cot_two = 0.5 * final_adjoint + cot_back
    cot_one, grad_one = adjoint_section(state_one, 0.5 * cot_two, primary_arrhenius_exponent, cell_kinds)
    cot_first, grad_zero = adjoint_section(state_zero, cot_one, primary_arrhenius_exponent, cell_kinds)
    adjoint_start = 0.5 * cot_two + cot_first
    rate_gradient = grad_three + grad_two + grad_one + grad_zero
    return (adjoint_start, rate_gradient)
```

```python
import jax
import jax.numpy as jnp
from jax import lax
from jax.experimental import pallas as pl
from jax.experimental.pallas import tpu as pltpu
from jax.sharding import PartitionSpec as P

GAMMA1 = 0.3
DT = 0.06
E0 = 1.0 / 0.3 + 0.32

R = 4
NROW = 2 + 2 * R
NF = 10
BLK = 104
SLOTS, STRIDE, HALO = 4, 36, 6
CR = ("cross", "role")
F32 = jnp.float32


def iota_lane():
    return lax.broadcasted_iota(jnp.int32, (1, 8, 128), 2)


def rl(x, shift):
    shift %= 128
    return x if shift == 0 else pltpu.roll(x, shift, axis=x.ndim - 1)


def lane_p(x):
    return pltpu.roll(x, 127, axis=2)


def lane_m(x):
    return pltpu.roll(x, 1, axis=2)


def axial_p(x, sub):
    r = pltpu.roll(x, 7, axis=1)
    return jnp.where(sub == 7, jnp.concatenate([r[1:], x[1:]], axis=0), r)


def axial_m(x, sub):
    r = pltpu.roll(x, 1, axis=1)
    return jnp.where(sub == 0, jnp.concatenate([x[:1], r[:1]], axis=0), r)


def primitives(q, rate):
    r = 1.0 / q[0]
    u = [q[1] * r, q[2] * r, q[3] * r]
    kin = 0.5 * (q[1] * u[0] + q[2] * u[1] + q[3] * u[2])
    p = GAMMA1 * (q[4] - kin)
    inv_t = q[0] / p
    e1 = DT * jnp.exp(rate - inv_t)
    e2 = (2.0 * DT) * jnp.exp(-1.5 * inv_t)
    return r, u, p, inv_t, e1, e2


def relax(kind):
    return jnp.where(kind == 1.0, 2.0 * DT, 0.0), jnp.where(kind == 2.0, DT, 0.0)


def forward_row(q, rate, kind, sub):
    r, u, p, inv_t, e1, e2 = primitives(q, rate)
    ri, rs = relax(kind)
    w1 = e1 * q[5]
    w2 = e2 * q[6]
    hp = (0.5 * DT) * p
    ce = (1.0 - 12.0 * DT) - ri
    cm = ce - rs
    acc = [q[k] * (cm if k in (1, 2, 3) else ce) for k in range(8)]
    acc[0] = acc[0] + ri
    acc[1] = acc[1] + 0.8 * ri
    acc[4] = acc[4] + E0 * ri + (3.0 * w1 + 2.0 * w2)
    acc[5] = acc[5] + ri - w1
    acc[6] = acc[6] + (w1 - w2)
    acc[7] = acc[7] + w2
    radial = None
    for d in range(3):
        h = (0.5 * DT) * u[d]
        ha = h - 2.0 * DT
        hb = h + 2.0 * DT
        a = [q[k] * ha for k in range(8)]
        b = [q[k] * hb for k in range(8)]
        pu = hp * u[d]
        a[d + 1] = a[d + 1] + hp
        b[d + 1] = b[d + 1] + hp
        a[4] = a[4] + pu
        b[4] = b[4] + pu
        if d == 1:
            radial = (a, b)
        elif d == 0:
            acc = [acc[k] - axial_p(a[k], sub) + axial_m(b[k], sub) for k in range(8)]
        else:
            acc = [acc[k] - lane_p(a[k]) + lane_m(b[k]) for k in range(8)]
    return acc, radial[0], radial[1]


def adjoint_row(q, rate, kind, c, cp, cm, bz, sub, bax):
    r, u, p, inv_t, e1, e2 = primitives(q, rate)
    ri, rs = relax(kind)
    al1 = 3.0 * c[4] - c[5] + c[6]
    al2 = 2.0 * c[4] - c[6] + c[7]
    g1 = e1 * al1
    g2 = e2 * al2
    rate_grad = g1 * q[5]
    gg = (rate_grad + 1.5 * (g2 * q[6])) * inv_t
    ce = (1.0 - 12.0 * DT) - ri
    cmo = ce - rs
    out = [c[k] * (cmo if k in (1, 2, 3) else ce) for k in range(8)]
    out[5] = out[5] + g1
    out[6] = out[6] + g2
    gp = gg * inv_t * r
    rho = -gg * r
    total = [None] * 8
    for d in range(3):
        if d == 0:
            hi = [axial_p(c[k], sub) for k in range(8)]
            lo = [axial_m(c[k], sub) for k in range(8)]
            w = [(hi[k] - lo[k]) + bax * c[k] for k in range(8)]
        elif d == 1:
            hi, lo = cp, cm
            w = [(hi[k] - lo[k]) + bz * c[k] for k in range(8)]
        else:
            hi = [lane_p(c[k]) for k in range(8)]
            lo = [lane_m(c[k]) for k in range(8)]
            w = [hi[k] - lo[k] for k in range(8)]
        total = [hi[k] + lo[k] if total[k] is None else total[k] + (hi[k] + lo[k]) for k in range(8)]
        h = (0.5 * DT) * u[d]
        s = q[0] * w[0]
        for k in range(1, 8):
            s = s + q[k] * w[k]
        s = ((0.5 * DT) * r) * (s + p * w[4])
        out = [out[k] + h * w[k] for k in range(8)]
        out[d + 1] = out[d + 1] + s
        rho = rho - s * u[d]
        gp = gp + ((0.5 * DT) * w[d + 1] + h * w[4])
    gp = GAMMA1 * gp
    rho = rho + (0.5 * gp) * (u[0] * u[0] + u[1] * u[1] + u[2] * u[2])
    out[0] = out[0] + rho
    for j in range(3):
        out[j + 1] = out[j + 1] - gp * u[j]
    out[4] = out[4] + gp
    return [out[k] + (2.0 * DT) * total[k] for k in range(8)], rate_grad


def sub_index():
    return lax.broadcasted_iota(jnp.int32, (1, 8, 128), 1)


def axial_mend():
    t = lax.broadcasted_iota(jnp.int32, (2, 8, 128), 0)
    s = lax.broadcasted_iota(jnp.int32, (2, 8, 128), 1)
    return jnp.where((t == 1) & (s == 7), -2.0, jnp.where((t == 0) & (s == 0), 2.0, 0.0))


def radial_ends():
    pos = lax.axis_index("cross") * lax.axis_size("role") + lax.axis_index("role")
    count = lax.axis_size("cross") * lax.axis_size("role")
    first = R - 2 * pos
    last = R + 2 * (count - pos) - 1
    return first, last


def scalar_mend(j, first, last):
    return jnp.where(j == last, -2.0, jnp.where(j == first, 2.0, 0.0)).astype(F32)


def edge_rows(s):
    lane = iota_lane()
    pack = jnp.where(lane >= 2 * STRIDE, 2, jnp.where(lane >= STRIDE, 1, 0))
    return pack * SLOTS + s


def lane_between(a, b):
    lane = iota_lane()
    return (lane >= a) & (lane < b)


def build_kernel(x_ref, rate_ref, kind_ref, out_ref, pad_ref):
    n = out_ref.shape[0]
    rows = 2 * n
    for f in range(NF):
        v = x_ref[f, 0] if f < 8 else (rate_ref[0] if f == 8 else kind_ref[0].astype(F32))
        pad_ref[f, R : R + rows] = v
        pad_ref[f, 0:R] = jnp.broadcast_to(v[0:1], (R, 128))
        pad_ref[f, R + rows : 2 * R + rows] = jnp.broadcast_to(v[rows - 1 : rows], (R, 128))
    for d in range(n):
        for f in range(NF):
            out_ref[d, f * NROW : (f + 1) * NROW] = pad_ref[f, 2 * d : 2 * d + NROW]
        out_ref[d, NF * NROW :] = jnp.zeros((BLK - NF * NROW, 128), F32)


def spread_kernel(recv_ref, fa_ref, fal_ref, far_ref, s0_ref, f_ref, e_ref, fe_ref, left_ref, right_ref):
    def edges(v, j, fi, own, ri):
        p, s = j // SLOTS, j % SLOTS
        base = STRIDE * p
        a = rl(v, base + HALO)
        b = rl(v, base + 3 * HALO - (128 - 2 * HALO))
        m = lane_between(base + HALO, base + 3 * HALO)
        m2 = lane_between(base + HALO, base + 5 * HALO)
        w = jnp.where(m, a, b)
        own[s] = w if own[s] is None else jnp.where(m2, w, own[s])
        k = base + HALO * s
        mk = lane_between(k, k + HALO)
        to_left = rl(v, k)
        to_right = rl(v, k + HALO - 128)
        ri[0] = to_left if ri[0] is None else jnp.where(mk, to_left, ri[0])
        ri[1] = to_right if ri[1] is None else jnp.where(mk, to_right, ri[1])

    for f in range(NF):
        own, sends = [None] * SLOTS, [None, None]
        for j in range(NROW):
            v = recv_ref[pl.ds(f * NROW + j, 16, stride=BLK), :].reshape(2, 8, 128)
            s0_ref[f, j] = v
            edges(v, j, f, own, sends)
        for s in range(SLOTS):
            e_ref[f, s] = own[s]
        left_ref[f], right_ref[f] = sends[0], sends[1]
    for f in range(8):
        own, sends = [None] * SLOTS, [None, None]
        for i in range(6):
            src = (fal_ref, fa_ref, far_ref)[i // 2]
            v = src[pl.ds(f * 32 + i % 2, 16, stride=2), :].reshape(2, 8, 128)
            f_ref[f, i] = v
            edges(v, i + 2, f, own, sends)
        for s in range(SLOTS):
            fe_ref[f, s] = own[s]
        left_ref[NF + f], right_ref[NF + f] = sends[0], sends[1]


def load(ref, j):
    return [ref[k, j] for k in range(8)]


def store(ref, j, v):
    for k in range(8):
        ref[k, j] = v[k]


def main_kernel(s0_ref, f_ref, c2_ref, s1_ref, kg_ref, st_ref, a_ref, b_ref, c3_ref):
    sub, bax = sub_index(), axial_mend()
    first, last = radial_ends()

    def level(src, dst, lo, hi, mix):
        def one(j, _):
            acc, a, b = forward_row(load(src, j), s0_ref[8, j], s0_ref[9, j], sub)
            store(a_ref, j, a)
            store(b_ref, j, b)
            store(dst, j, acc)
            return 0

        def two(j, _):
            jp = jnp.minimum(j + 1, jnp.maximum(last, j))
            jm = jnp.maximum(j - 1, jnp.minimum(first, j))
            jp = jnp.where(j == last, j, j + 1)
            jm = jnp.where(j == first, j, j - 1)
            for k in range(8):
                v = dst[k, j] - a_ref[k, jp] + b_ref[k, jm]
                if mix:
                    v = 0.5 * s0_ref[k, j] + 0.5 * v
                dst[k, j] = v
            return 0

        lax.fori_loop(lo - 1, hi + 2, one, 0)
        lax.fori_loop(lo, hi + 1, two, 0)

    st1, st2, st3 = st_ref.at[0], st_ref.at[1], st_ref.at[2]
    level(s0_ref, st1, 1, NROW - 2, False)
    level(st1, st2, 2, NROW - 3, True)
    level(st2, st3, 3, NROW - 4, False)

    def adj3(j, _):
        jp = jnp.where(j == last, j, j + 1) - 2
        jm = jnp.where(j == first, j, j - 1) - 2
        o, g = adjoint_row(
            load(st3, j), s0_ref[8, j], s0_ref[9, j], load(f_ref, j - 2), load(f_ref, jp), load(f_ref, jm),
            scalar_mend(j, first, last), sub, bax,
        )
        store(c3_ref, j - 3, [0.5 * v for v in o])
        a_ref[0, j] = 0.5 * g
        store(s1_ref, j - 3, load(st1, j))
        return 0

    lax.fori_loop(3, 7, adj3, 0)

    def adj2(j, _):
        jp = jnp.where(j == last, j, j + 1) - 3
        jm = jnp.where(j == first, j, j - 1) - 3
        o, g = adjoint_row(
            load(st2, j), s0_ref[8, j], s0_ref[9, j], load(c3_ref, j - 3), load(c3_ref, jp), load(c3_ref, jm),
            scalar_mend(j, first, last), sub, bax,
        )
        for k in range(8):
            c2_ref[k, j - 4] = 0.5 * f_ref[k, j - 2] + o[k]
        kg_ref[j - 4] = a_ref[0, j] + g
        return 0

    lax.fori_loop(4, 6, adj2, 0)


def wrap_slots(ref, k, s, v):
    ref[k, s + 1] = v
    if s == 0:
        ref[k, SLOTS + 1] = rl(v, -STRIDE)
    if s == SLOTS - 1:
        ref[k, 0] = rl(v, STRIDE)


def edge_mend(s, first, last):
    rows = edge_rows(s)
    return rows == first, rows == last


def edge_adjoint(state, e_ref, c_ref, s, first, last, sub, bax):
    mf, ml = edge_mend(s, first, last)
    c = load(c_ref, s + 1)
    cp = [jnp.where(ml, c[k], c_ref[k, s + 2]) for k in range(8)]
    cm = [jnp.where(mf, c[k], c_ref[k, s]) for k in range(8)]
    bz = jnp.where(ml, -2.0, jnp.where(mf, 2.0, 0.0))
    return adjoint_row(load(state, s), e_ref[8, s], e_ref[9, s], c, cp, cm, bz, sub, bax)


def edge_kernel(e_ref, fe_ref, fl_ref, fr_ref, c2_ref, c2s_ref, s1_ref, kg_ref, e0_ref, st_ref, a_ref, b_ref, c_ref, fx_ref):
    sub, bax = sub_index(), axial_mend()
    first, last = radial_ends()

    def halo(v, f, s):
        for p in range(3):
            base = STRIDE * p
            v = jnp.where(lane_between(base, base + HALO), rl(fl_ref[f], -HALO * s), v)
            v = jnp.where(lane_between(base + 5 * HALO, base + 6 * HALO), rl(fr_ref[f], HALO * (5 - s)), v)
        return v

    for f in range(NF):
        for s in range(SLOTS):
            e0_ref[f, s] = halo(e_ref[f, s], f, s)
    for f in range(8):
        for s in range(SLOTS):
            wrap_slots(fx_ref, f, s, halo(fe_ref[f, s], NF + f, s))

    def level(src, dst, mix):
        for s in range(SLOTS):
            acc, a, b = forward_row(load(src, s), e0_ref[8, s], e0_ref[9, s], sub)
            store(dst, s, acc)
            for k in range(8):
                wrap_slots(a_ref, k, s, a[k])
                wrap_slots(b_ref, k, s, b[k])
        for s in range(SLOTS):
            mf, ml = edge_mend(s, first, last)
            for k in range(8):
                ap = jnp.where(ml, a_ref[k, s + 1], a_ref[k, s + 2])
                bm = jnp.where(mf, b_ref[k, s + 1], b_ref[k, s])
                v = dst[k, s] - ap + bm
                if mix:
                    v = 0.5 * e0_ref[k, s] + 0.5 * v
                dst[k, s] = v

    st2, st3 = st_ref.at[0], st_ref.at[1]
    level(e0_ref, s1_ref, False)
    level(s1_ref, st2, True)
    level(st2, st3, False)
    g3 = []
    for s in range(SLOTS):
        o, g = edge_adjoint(st3, e0_ref, fx_ref, s, first, last, sub, bax)
        for k in range(8):
            wrap_slots(c_ref, k, s, 0.5 * o[k])
        g3.append(0.5 * g)
    second = lane_between(2 * STRIDE, 128)
    res = []
    for s in range(2):
        o, g = edge_adjoint(st2, e0_ref, c_ref, s, first, last, sub, bax)
        kg_ref[s] = g3[s] + g
        res.append([0.5 * fx_ref[k, s + 1] + o[k] for k in range(8)])
    for k in range(8):
        c2s_ref[k, 0] = c2_ref[k, 0]
        c2s_ref[k, 1] = c2_ref[k, 1]
        c2s_ref[k, 2] = jnp.where(second, rl(res[1][k], STRIDE), res[0][k])


def final_kernel(own_ref, lo_ref, hi_ref, s1_ref, s1e_ref, s0_ref, e0_ref, kg_ref, kge_ref, out_ref, rg_ref,
                 c2_ref, c1_ref, ce_ref, c1e_ref):
    sub, bax = sub_index(), axial_mend()
    first, last = radial_ends()
    for i, ref in enumerate((lo_ref, own_ref, hi_ref)):
        for k in range(8):
            c2_ref[k, 2 * i] = ref[k, 0]
            c2_ref[k, 2 * i + 1] = ref[k, 1]
    low = lane_between(0, STRIDE)
    for k in range(8):
        lo, own, hi = lo_ref[k, 2], own_ref[k, 2], hi_ref[k, 2]
        wrap_slots(ce_ref, k, 0, own)
        wrap_slots(ce_ref, k, 1, rl(own, -STRIDE))
        wrap_slots(ce_ref, k, 2, jnp.where(low, rl(lo, -STRIDE), hi))
        wrap_slots(ce_ref, k, 3, jnp.where(low, rl(lo, -2 * STRIDE), rl(hi, -STRIDE)))

    def adj1(j, _):
        jp = jnp.where(j == last, j, j + 1) - 2
        jm = jnp.where(j == first, j, j - 1) - 2
        o, g = adjoint_row(
            load(s1_ref, j - 3), s0_ref[8, j], s0_ref[9, j], load(c2_ref, j - 2), load(c2_ref, jp), load(c2_ref, jm),
            scalar_mend(j, first, last), sub, bax,
        )
        for k in range(8):
            c1_ref[k, j - 3] = 0.5 * o[k]
        c1_ref[8, j - 3] = 0.5 * g
        return 0

    lax.fori_loop(3, 7, adj1, 0)
    ge = []
    for s in range(SLOTS):
        o, g = edge_adjoint(s1e_ref, e0_ref, ce_ref, s, first, last, sub, bax)
        for k in range(8):
            wrap_slots(c1e_ref, k, s, 0.5 * o[k])
        ge.append(0.5 * g)

    head = lane_between(0, HALO)
    tail = lane_between(128 - HALO, 128)

    def merge(m, e):
        return jnp.where(head, rl(e, -(STRIDE + HALO)), jnp.where(tail, rl(e, 128 - HALO - (STRIDE + 4 * HALO)), m))

    for s in range(2):
        j = s + R
        jp = jnp.where(j == last, j, j + 1) - 3
        jm = jnp.where(j == first, j, j - 1) - 3
        o, g = adjoint_row(
            load(s0_ref, j), s0_ref[8, j], s0_ref[9, j], load(c1_ref, j - 3), load(c1_ref, jp), load(c1_ref, jm),
            scalar_mend(j, first, last), sub, bax,
        )
        oe, gedge = edge_adjoint(e0_ref, e0_ref, c1e_ref, s, first, last, sub, bax)
        for k in range(8):
            v = merge(0.5 * c2_ref[k, j - 2] + o[k], 0.5 * ce_ref[k, s + 1] + oe[k])
            out_ref[pl.ds(k * 32 + s, 16, stride=2), :] = v.reshape(16, 128)
        v = merge(kg_ref[s] + c1_ref[8, j - 3] + g, kge_ref[s] + ge[s] + gedge)
        rg_ref[pl.ds(s, 16, stride=2), :] = v.reshape(16, 128)


def call(kernel, outs, scratch, *args):
    return pl.pallas_call(
        kernel,
        out_shape=[jax.ShapeDtypeStruct(o, F32) for o in outs],
        in_specs=[pl.BlockSpec(memory_space=pltpu.VMEM)] * len(args),
        out_specs=[pl.BlockSpec(memory_space=pltpu.VMEM)] * len(outs),
        scratch_shapes=[pltpu.VMEM(s, F32) for s in scratch],
    )(*args)


T = (2, 8, 128)


def shifted(x, axis, step, ring):
    n = lax.axis_size(axis)
    pairs = [(i, (i + step) % n) for i in range(n) if ring or 0 <= i + step < n]
    return lax.ppermute(x, axis, pairs)


def shards(checkpoint, rate, kinds, final_adjoint):
    n = lax.axis_size(CR)
    fa = final_adjoint.reshape(256, 128)
    fal = shifted(fa, CR, 1, False)
    far = shifted(fa, CR, -1, False)
    (send,) = call(build_kernel, [(n, BLK, 128)], [(NF, 2 * n + 2 * R, 128)], checkpoint, rate, kinds)
    recv = lax.all_to_all(send, CR, split_axis=0, concat_axis=0, tiled=True)
    s0, f, e, fe, left, right = call(
        spread_kernel,
        [(NF, NROW) + T, (8, 6) + T, (NF, SLOTS) + T, (8, SLOTS) + T, (NF + 8,) + T, (NF + 8,) + T],
        [],
        recv.reshape(n * BLK, 128), fa, fal, far,
    )
    from_right = shifted(left, "azim", -1, True)
    from_left = shifted(right, "azim", 1, True)
    c2, s1, kg = call(
        main_kernel,
        [(8, 2) + T, (8, 4) + T, (2,) + T],
        [(3, 8, NROW) + T, (8, NROW) + T, (8, NROW) + T, (8, 4) + T],
        s0, f,
    )
    c2s, s1e, kge, e0 = call(
        edge_kernel,
        [(8, 3) + T, (8, SLOTS) + T, (2,) + T, (NF, SLOTS) + T],
        [(2, 8, SLOTS) + T] + [(8, SLOTS + 2) + T] * 4,
        e, fe, from_left, from_right, c2,
    )
    lo = shifted(c2s, CR, 1, False)
    hi = shifted(c2s, CR, -1, False)
    out, rg = call(
        final_kernel,
        [(256, 128), (32, 128)],
        [(8, 6) + T, (9, 4) + T, (8, SLOTS + 2) + T, (8, SLOTS + 2) + T],
        c2s, lo, hi, s1, s1e, s0, e0, kg, kge,
    )
    return out.reshape(8, 16, 2, 128), rg.reshape(16, 2, 128)


def solution(mesh):
    return jax.shard_map(
        shards,
        mesh=mesh,
        in_specs=(
            P(None, CR, None, "azim"),
            P(CR, None, "azim"),
            P(CR, None, "azim"),
            P(None, None, CR, "azim"),
        ),
        out_specs=(P(None, None, CR, "azim"), P(None, CR, "azim")),
        check_vma=False,
    )
```

```python
import jax
import jax.numpy as jnp
from jax import lax
from jax.experimental import pallas as pl
from jax.experimental.pallas import tpu as pltpu
from jax.sharding import PartitionSpec as P

GAMMA1 = 0.3
DT = 0.06
E0 = 1.0 / 0.3 + 0.32

R = 4
NROW = 2 + 2 * R
NF = 10
BLK = 104
SLOTS, STRIDE, HALO = 4, 36, 6
CR = ("cross", "role")
F32 = jnp.float32


def iota_lane():
    return lax.broadcasted_iota(jnp.int32, (1, 8, 128), 2)


def rl(x, shift):
    shift %= 128
    return x if shift == 0 else pltpu.roll(x, shift, axis=x.ndim - 1)


def lane_p(x):
    return pltpu.roll(x, 127, axis=2)


def lane_m(x):
    return pltpu.roll(x, 1, axis=2)


def axial_p(x, sub):
    r = pltpu.roll(x, 7, axis=1)
    return jnp.where(sub == 7, jnp.concatenate([r[1:], x[1:]], axis=0), r)


def axial_m(x, sub):
    r = pltpu.roll(x, 1, axis=1)
    return jnp.where(sub == 0, jnp.concatenate([x[:1], r[:1]], axis=0), r)


def primitives(q, rate):
    r = 1.0 / q[0]
    u = [q[1] * r, q[2] * r, q[3] * r]
    kin = 0.5 * (q[1] * u[0] + q[2] * u[1] + q[3] * u[2])
    p = GAMMA1 * (q[4] - kin)
    inv_t = q[0] / p
    e1 = DT * jnp.exp(rate - inv_t)
    e2 = (2.0 * DT) * jnp.exp(-1.5 * inv_t)
    return r, u, p, inv_t, e1, e2


def relax(kind):
    return jnp.where(kind == 1.0, 2.0 * DT, 0.0), jnp.where(kind == 2.0, DT, 0.0)


def forward_row(q, rate, kind, sub):
    r, u, p, inv_t, e1, e2 = primitives(q, rate)
    ri, rs = relax(kind)
    w1 = e1 * q[5]
    w2 = e2 * q[6]
    hp = (0.5 * DT) * p
    ce = (1.0 - 12.0 * DT) - ri
    cm = ce - rs
    acc = [q[k] * (cm if k in (1, 2, 3) else ce) for k in range(8)]
    acc[0] = acc[0] + ri
    acc[1] = acc[1] + 0.8 * ri
    acc[4] = acc[4] + E0 * ri + (3.0 * w1 + 2.0 * w2)
    acc[5] = acc[5] + ri - w1
    acc[6] = acc[6] + (w1 - w2)
    acc[7] = acc[7] + w2
    radial = None
    for d in range(3):
        h = (0.5 * DT) * u[d]
        ha = h - 2.0 * DT
        hb = h + 2.0 * DT
        a = [q[k] * ha for k in range(8)]
        b = [q[k] * hb for k in range(8)]
        pu = hp * u[d]
        a[d + 1] = a[d + 1] + hp
        b[d + 1] = b[d + 1] + hp
        a[4] = a[4] + pu
        b[4] = b[4] + pu
        if d == 1:
            radial = (a, b)
        elif d == 0:
            acc = [acc[k] - axial_p(a[k], sub) + axial_m(b[k], sub) for k in range(8)]
        else:
            acc = [acc[k] - lane_p(a[k]) + lane_m(b[k]) for k in range(8)]
    return acc, radial[0], radial[1]


def adjoint_row(q, rate, kind, c, cp, cm, bz, sub, bax):
    r, u, p, inv_t, e1, e2 = primitives(q, rate)
    ri, rs = relax(kind)
    al1 = 3.0 * c[4] - c[5] + c[6]
    al2 = 2.0 * c[4] - c[6] + c[7]
    g1 = e1 * al1
    g2 = e2 * al2
    rate_grad = g1 * q[5]
    gg = (rate_grad + 1.5 * (g2 * q[6])) * inv_t
    ce = (1.0 - 12.0 * DT) - ri
    cmo = ce - rs
    out = [c[k] * (cmo if k in (1, 2, 3) else ce) for k in range(8)]
    out[5] = out[5] + g1
    out[6] = out[6] + g2
    gp = gg * inv_t * r
    rho = -gg * r
    total = [None] * 8
    for d in range(3):
        if d == 0:
            hi = [axial_p(c[k], sub) for k in range(8)]
            lo = [axial_m(c[k], sub) for k in range(8)]
            w = [(hi[k] - lo[k]) + bax * c[k] for k in range(8)]
        elif d == 1:
            hi, lo = cp, cm
            w = [(hi[k] - lo[k]) + bz * c[k] for k in range(8)]
        else:
            hi = [lane_p(c[k]) for k in range(8)]
            lo = [lane_m(c[k]) for k in range(8)]
            w = [hi[k] - lo[k] for k in range(8)]
        total = [hi[k] + lo[k] if total[k] is None else total[k] + (hi[k] + lo[k]) for k in range(8)]
        h = (0.5 * DT) * u[d]
        s = q[0] * w[0]
        for k in range(1, 8):
            s = s + q[k] * w[k]
        s = ((0.5 * DT) * r) * (s + p * w[4])
        out = [out[k] + h * w[k] for k in range(8)]
        out[d + 1] = out[d + 1] + s
        rho = rho - s * u[d]
        gp = gp + ((0.5 * DT) * w[d + 1] + h * w[4])
    gp = GAMMA1 * gp
    rho = rho + (0.5 * gp) * (u[0] * u[0] + u[1] * u[1] + u[2] * u[2])
    out[0] = out[0] + rho
    for j in range(3):
        out[j + 1] = out[j + 1] - gp * u[j]
    out[4] = out[4] + gp
    return [out[k] + (2.0 * DT) * total[k] for k in range(8)], rate_grad


def sub_index():
    return lax.broadcasted_iota(jnp.int32, (1, 8, 128), 1)


def axial_mend():
    t = lax.broadcasted_iota(jnp.int32, (2, 8, 128), 0)
    s = lax.broadcasted_iota(jnp.int32, (2, 8, 128), 1)
    return jnp.where((t == 1) & (s == 7), -2.0, jnp.where((t == 0) & (s == 0), 2.0, 0.0))


def radial_ends():
    pos = lax.axis_index("cross") * lax.axis_size("role") + lax.axis_index("role")
    count = lax.axis_size("cross") * lax.axis_size("role")
    first = R - 2 * pos
    last = R + 2 * (count - pos) - 1
    return first, last


def scalar_mend(j, first, last):
    return jnp.where(j == last, -2.0, jnp.where(j == first, 2.0, 0.0)).astype(F32)


def edge_rows(s):
    lane = iota_lane()
    pack = jnp.where(lane >= 2 * STRIDE, 2, jnp.where(lane >= STRIDE, 1, 0))
    return pack * SLOTS + s


def lane_between(a, b):
    lane = iota_lane()
    return (lane >= a) & (lane < b)


def build_kernel(x_ref, rate_ref, kind_ref, out_ref, pad_ref):
    n = out_ref.shape[0]
    rows = 2 * n
    for f in range(NF):
        v = x_ref[f, 0] if f < 8 else (rate_ref[0] if f == 8 else kind_ref[0].astype(F32))
        pad_ref[f, R : R + rows] = v
        pad_ref[f, 0:R] = jnp.broadcast_to(v[0:1], (R, 128))
        pad_ref[f, R + rows : 2 * R + rows] = jnp.broadcast_to(v[rows - 1 : rows], (R, 128))
    for d in range(n):
        for f in range(NF):
            out_ref[d, f * NROW : (f + 1) * NROW] = pad_ref[f, 2 * d : 2 * d + NROW]
        out_ref[d, NF * NROW :] = jnp.zeros((BLK - NF * NROW, 128), F32)


def spread_kernel(recv_ref, fa_ref, fal_ref, far_ref, s0_ref, f_ref, e_ref, fe_ref, left_ref, right_ref):
    def edges(v, j, fi, own, ri):
        p, s = j // SLOTS, j % SLOTS
        base = STRIDE * p
        a = rl(v, base + HALO)
        b = rl(v, base + 3 * HALO - (128 - 2 * HALO))
        m = lane_between(base + HALO, base + 3 * HALO)
        m2 = lane_between(base + HALO, base + 5 * HALO)
        w = jnp.where(m, a, b)
        own[s] = w if own[s] is None else jnp.where(m2, w, own[s])
        k = base + HALO * s
        mk = lane_between(k, k + HALO)
        to_left = rl(v, k)
        to_right = rl(v, k + HALO - 128)
        ri[0] = to_left if ri[0] is None else jnp.where(mk, to_left, ri[0])
        ri[1] = to_right if ri[1] is None else jnp.where(mk, to_right, ri[1])

    for f in range(NF):
        own, sends = [None] * SLOTS, [None, None]
        for j in range(NROW):
            v = recv_ref[pl.ds(f * NROW + j, 16, stride=BLK), :].reshape(2, 8, 128)
            s0_ref[f, j] = v
            edges(v, j, f, own, sends)
        for s in range(SLOTS):
            e_ref[f, s] = own[s]
        left_ref[f], right_ref[f] = sends[0], sends[1]
    for f in range(8):
        own, sends = [None] * SLOTS, [None, None]
        for i in range(6):
            src = (fal_ref, fa_ref, far_ref)[i // 2]
            v = src[pl.ds(f * 32 + i % 2, 16, stride=2), :].reshape(2, 8, 128)
            f_ref[f, i] = v
            edges(v, i + 2, f, own, sends)
        for s in range(SLOTS):
            fe_ref[f, s] = own[s]
        left_ref[NF + f], right_ref[NF + f] = sends[0], sends[1]


def load(ref, j):
    return [ref[k, j] for k in range(8)]


def store(ref, j, v):
    for k in range(8):
        ref[k, j] = v[k]


def main_kernel(s0_ref, f_ref, c2_ref, s1_ref, kg_ref, st_ref, a_ref, b_ref, c3_ref):
    sub, bax = sub_index(), axial_mend()
    first, last = radial_ends()

    def level(src, dst, lo, hi, mix):
        def one(j, _):
            acc, a, b = forward_row(load(src, j), s0_ref[8, j], s0_ref[9, j], sub)
            store(a_ref, j, a)
            store(b_ref, j, b)
            store(dst, j, acc)
            return 0

        def two(j, _):
            jp = jnp.minimum(j + 1, jnp.maximum(last, j))
            jm = jnp.maximum(j - 1, jnp.minimum(first, j))
            jp = jnp.where(j == last, j, j + 1)
            jm = jnp.where(j == first, j, j - 1)
            for k in range(8):
                v = dst[k, j] - a_ref[k, jp] + b_ref[k, jm]
                if mix:
                    v = 0.5 * s0_ref[k, j] + 0.5 * v
                dst[k, j] = v
            return 0

        lax.fori_loop(lo - 1, hi + 2, one, 0)
        lax.fori_loop(lo, hi + 1, two, 0)

    st1, st2, st3 = st_ref.at[0], st_ref.at[1], st_ref.at[2]
    level(s0_ref, st1, 1, NROW - 2, False)
    level(st1, st2, 2, NROW - 3, True)
    level(st2, st3, 3, NROW - 4, False)

    def adj3(j, _):
        jp = jnp.where(j == last, j, j + 1) - 2
        jm = jnp.where(j == first, j, j - 1) - 2
        o, g = adjoint_row(
            load(st3, j), s0_ref[8, j], s0_ref[9, j], load(f_ref, j - 2), load(f_ref, jp), load(f_ref, jm),
            scalar_mend(j, first, last), sub, bax,
        )
        store(c3_ref, j - 3, [0.5 * v for v in o])
        a_ref[0, j] = 0.5 * g
        store(s1_ref, j - 3, load(st1, j))
        return 0

    lax.fori_loop(3, 7, adj3, 0)

    def adj2(j, _):
        jp = jnp.where(j == last, j, j + 1) - 3
        jm = jnp.where(j == first, j, j - 1) - 3
        o, g = adjoint_row(
            load(st2, j), s0_ref[8, j], s0_ref[9, j], load(c3_ref, j - 3), load(c3_ref, jp), load(c3_ref, jm),
            scalar_mend(j, first, last), sub, bax,
        )
        for k in range(8):
            c2_ref[k, j - 4] = 0.5 * f_ref[k, j - 2] + o[k]
        kg_ref[j - 4] = a_ref[0, j] + g
        return 0

    lax.fori_loop(4, 6, adj2, 0)


def wrap_slots(ref, k, s, v):
    ref[k, s + 1] = v
    if s == 0:
        ref[k, SLOTS + 1] = rl(v, -STRIDE)
    if s == SLOTS - 1:
        ref[k, 0] = rl(v, STRIDE)


def edge_mend(s, first, last):
    rows = edge_rows(s)
    return rows == first, rows == last


def edge_adjoint(state, e_ref, c_ref, s, first, last, sub, bax):
    mf, ml = edge_mend(s, first, last)
    c = load(c_ref, s + 1)
    cp = [jnp.where(ml, c[k], c_ref[k, s + 2]) for k in range(8)]
    cm = [jnp.where(mf, c[k], c_ref[k, s]) for k in range(8)]
    bz = jnp.where(ml, -2.0, jnp.where(mf, 2.0, 0.0))
    return adjoint_row(load(state, s), e_ref[8, s], e_ref[9, s], c, cp, cm, bz, sub, bax)


def edge_kernel(e_ref, fe_ref, fl_ref, fr_ref, c2_ref, c2s_ref, s1_ref, kg_ref, e0_ref, st_ref, a_ref, b_ref, c_ref, fx_ref):
    sub, bax = sub_index(), axial_mend()
    first, last = radial_ends()

    def halo(v, f, s):
        for p in range(3):
            base = STRIDE * p
            v = jnp.where(lane_between(base, base + HALO), rl(fl_ref[f], -HALO * s), v)
            v = jnp.where(lane_between(base + 5 * HALO, base + 6 * HALO), rl(fr_ref[f], HALO * (5 - s)), v)
        return v

    for f in range(NF):
        for s in range(SLOTS):
            e0_ref[f, s] = halo(e_ref[f, s], f, s)
    for f in range(8):
        for s in range(SLOTS):
            wrap_slots(fx_ref, f, s, halo(fe_ref[f, s], NF + f, s))

    def level(src, dst, mix):
        for s in range(SLOTS):
            acc, a, b = forward_row(load(src, s), e0_ref[8, s], e0_ref[9, s], sub)
            store(dst, s, acc)
            for k in range(8):
                wrap_slots(a_ref, k, s, a[k])
                wrap_slots(b_ref, k, s, b[k])
        for s in range(SLOTS):
            mf, ml = edge_mend(s, first, last)
            for k in range(8):
                ap = jnp.where(ml, a_ref[k, s + 1], a_ref[k, s + 2])
                bm = jnp.where(mf, b_ref[k, s + 1], b_ref[k, s])
                v = dst[k, s] - ap + bm
                if mix:
                    v = 0.5 * e0_ref[k, s] + 0.5 * v
                dst[k, s] = v

    st2, st3 = st_ref.at[0], st_ref.at[1]
    level(e0_ref, s1_ref, False)
    level(s1_ref, st2, True)
    level(st2, st3, False)
    g3 = []
    for s in range(SLOTS):
        o, g = edge_adjoint(st3, e0_ref, fx_ref, s, first, last, sub, bax)
        for k in range(8):
            wrap_slots(c_ref, k, s, 0.5 * o[k])
        g3.append(0.5 * g)
    second = lane_between(2 * STRIDE, 128)
    res = []
    for s in range(2):
        o, g = edge_adjoint(st2, e0_ref, c_ref, s, first, last, sub, bax)
        kg_ref[s] = g3[s] + g
        res.append([0.5 * fx_ref[k, s + 1] + o[k] for k in range(8)])
    for k in range(8):
        c2s_ref[k, 0] = c2_ref[k, 0]
        c2s_ref[k, 1] = c2_ref[k, 1]
        c2s_ref[k, 2] = jnp.where(second, rl(res[1][k], STRIDE), res[0][k])


def final_kernel(own_ref, lo_ref, hi_ref, s1_ref, s1e_ref, s0_ref, e0_ref, kg_ref, kge_ref, out_ref, rg_ref,
                 c2_ref, c1_ref, ce_ref, c1e_ref):
    sub, bax = sub_index(), axial_mend()
    first, last = radial_ends()
    for i, ref in enumerate((lo_ref, own_ref, hi_ref)):
        for k in range(8):
            c2_ref[k, 2 * i] = ref[k, 0]
            c2_ref[k, 2 * i + 1] = ref[k, 1]
    low = lane_between(0, STRIDE)
    for k in range(8):
        lo, own, hi = lo_ref[k, 2], own_ref[k, 2], hi_ref[k, 2]
        wrap_slots(ce_ref, k, 0, own)
        wrap_slots(ce_ref, k, 1, rl(own, -STRIDE))
        wrap_slots(ce_ref, k, 2, jnp.where(low, rl(lo, -STRIDE), hi))
        wrap_slots(ce_ref, k, 3, jnp.where(low, rl(lo, -2 * STRIDE), rl(hi, -STRIDE)))

    def adj1(j, _):
        jp = jnp.where(j == last, j, j + 1) - 2
        jm = jnp.where(j == first, j, j - 1) - 2
        o, g = adjoint_row(
            load(s1_ref, j - 3), s0_ref[8, j], s0_ref[9, j], load(c2_ref, j - 2), load(c2_ref, jp), load(c2_ref, jm),
            scalar_mend(j, first, last), sub, bax,
        )
        for k in range(8):
            c1_ref[k, j - 3] = 0.5 * o[k]
        c1_ref[8, j - 3] = 0.5 * g
        return 0

    lax.fori_loop(3, 7, adj1, 0)
    ge = []
    for s in range(SLOTS):
        o, g = edge_adjoint(s1e_ref, e0_ref, ce_ref, s, first, last, sub, bax)
        for k in range(8):
            wrap_slots(c1e_ref, k, s, 0.5 * o[k])
        ge.append(0.5 * g)

    head = lane_between(0, HALO)
    tail = lane_between(128 - HALO, 128)

    def merge(m, e):
        return jnp.where(head, rl(e, -(STRIDE + HALO)), jnp.where(tail, rl(e, 128 - HALO - (STRIDE + 4 * HALO)), m))

    for s in range(2):
        j = s + R
        jp = jnp.where(j == last, j, j + 1) - 3
        jm = jnp.where(j == first, j, j - 1) - 3
        o, g = adjoint_row(
            load(s0_ref, j), s0_ref[8, j], s0_ref[9, j], load(c1_ref, j - 3), load(c1_ref, jp), load(c1_ref, jm),
            scalar_mend(j, first, last), sub, bax,
        )
        oe, gedge = edge_adjoint(e0_ref, e0_ref, c1e_ref, s, first, last, sub, bax)
        for k in range(8):
            v = merge(0.5 * c2_ref[k, j - 2] + o[k], 0.5 * ce_ref[k, s + 1] + oe[k])
            out_ref[pl.ds(k * 32 + s, 16, stride=2), :] = v.reshape(16, 128)
        v = merge(kg_ref[s] + c1_ref[8, j - 3] + g, kge_ref[s] + ge[s] + gedge)
        rg_ref[pl.ds(s, 16, stride=2), :] = v.reshape(16, 128)


def call(kernel, outs, scratch, *args, near=True, leave=False):
    args = [pltpu.with_memory_space_constraint(a, pltpu.VMEM if near else pltpu.HBM) for a in args]
    return pl.pallas_call(
        kernel,
        out_shape=[jax.ShapeDtypeStruct(o, F32) if leave else pltpu.VMEM(o, F32) for o in outs],
        in_specs=[pl.BlockSpec(memory_space=pltpu.VMEM)] * len(args),
        out_specs=[pl.BlockSpec(memory_space=pltpu.VMEM)] * len(outs),
        scratch_shapes=[pltpu.VMEM(s, F32) for s in scratch],
        compiler_params=pltpu.CompilerParams(vmem_limit_bytes=8 * 1024 * 1024),
    )(*args)


T = (2, 8, 128)


def shifted(x, axis, step):
    n = lax.axis_size(axis)
    return lax.ppermute(x, axis, [(i, (i + step) % n) for i in range(n)])


def shards(checkpoint, rate, kinds, final_adjoint):
    n = lax.axis_size(CR)
    fa = final_adjoint.reshape(256, 128)
    fal = shifted(fa, CR, 1)
    far = shifted(fa, CR, -1)
    (send,) = call(build_kernel, [(n, BLK, 128)], [(NF, 2 * n + 2 * R, 128)], checkpoint, rate, kinds, near=False, leave=True)
    recv = lax.all_to_all(send, CR, split_axis=0, concat_axis=0, tiled=True)
    s0, f, e, fe, left, right = call(
        spread_kernel,
        [(NF, NROW) + T, (8, 6) + T, (NF, SLOTS) + T, (8, SLOTS) + T, (NF + 8,) + T, (NF + 8,) + T],
        [],
        recv.reshape(n * BLK, 128), fa, fal, far,
    )
    from_right = shifted(left, "azim", -1)
    from_left = shifted(right, "azim", 1)
    c2, s1, kg = call(
        main_kernel,
        [(8, 2) + T, (8, 4) + T, (2,) + T],
        [(3, 8, NROW) + T, (8, NROW) + T, (8, NROW) + T, (8, 4) + T],
        s0, f,
    )
    c2s, s1e, kge, e0 = call(
        edge_kernel,
        [(8, 3) + T, (8, SLOTS) + T, (2,) + T, (NF, SLOTS) + T],
        [(2, 8, SLOTS) + T] + [(8, SLOTS + 2) + T] * 4,
        e, fe, from_left, from_right, c2,
    )
    lo = shifted(c2s, CR, 1)
    hi = shifted(c2s, CR, -1)
    out, rg = call(
        final_kernel,
        [(256, 128), (32, 128)],
        [(8, 6) + T, (9, 4) + T, (8, SLOTS + 2) + T, (8, SLOTS + 2) + T],
        c2s, lo, hi, s1, s1e, s0, e0, kg, kge, leave=True,
    )
    return out.reshape(8, 16, 2, 128), rg.reshape(16, 2, 128)


def solution(mesh):
    return jax.shard_map(
        shards,
        mesh=mesh,
        in_specs=(
            P(None, CR, None, "azim"),
            P(CR, None, "azim"),
            P(CR, None, "azim"),
            P(None, None, CR, "azim"),
        ),
        out_specs=(P(None, None, CR, "azim"), P(None, CR, "azim")),
        check_vma=False,
    )
```

```python
import jax
import jax.numpy as jnp
from jax import lax
from jax.experimental import pallas as pl
from jax.experimental.pallas import tpu as pltpu
from jax.sharding import PartitionSpec as P


GAMMA1 = 0.3
DT = 0.06
E0 = 1.0 / 0.3 + 0.32

R = 6
RF = 4
NROW = 2 + 2 * R
NFA = 2 + 2 * RF
CHIP = NROW + 2
NF = 10
BLK = NF * CHIP
SLOTS, STRIDE, HALO = 5, 36, 6
CR = ("cross", "role")
F32 = jnp.float32


def iota_lane():
    return lax.broadcasted_iota(jnp.int32, (1, 8, 128), 2)


def rl(x, shift):
    shift %= 128
    return x if shift == 0 else pltpu.roll(x, shift, axis=x.ndim - 1)


def lane_p(x):
    return pltpu.roll(x, 127, axis=2)


def lane_m(x):
    return pltpu.roll(x, 1, axis=2)


def axial_p(x, sub):
    return jnp.concatenate([x[1:], jnp.where(sub == 7, x[1:], pltpu.roll(x[:1], 7, axis=1))], axis=0)


def axial_m(x, sub):
    return jnp.concatenate([jnp.where(sub == 0, x[:1], pltpu.roll(x[1:], 1, axis=1)), x[:1]], axis=0)


def primitives(q, rate):
    r = 1.0 / q[0]
    u = [q[1] * r, q[2] * r, q[3] * r]
    kin = 0.5 * (q[1] * u[0] + q[2] * u[1] + q[3] * u[2])
    p = GAMMA1 * (q[4] - kin)
    inv_t = q[0] / p
    e1 = DT * jnp.exp(rate - inv_t)
    e2 = (2.0 * DT) * jnp.exp(-1.5 * inv_t)
    return r, u, p, inv_t, e1, e2


def relax(kind):
    return jnp.where(kind == 1.0, 2.0 * DT, 0.0), jnp.where(kind == 2.0, DT, 0.0)


def forward_row(q, rate, kind, sub):
    _, u, p, _, e1, e2 = primitives(q, rate)
    ri, rs = relax(kind)
    w1 = e1 * q[5]
    w2 = e2 * q[6]
    hp = (0.5 * DT) * p
    ce = (1.0 - 12.0 * DT) - ri
    cm = ce - rs
    acc = [q[k] * (cm if k in (1, 2, 3) else ce) for k in range(8)]
    acc[0] = acc[0] + ri
    acc[1] = acc[1] + 0.8 * ri
    acc[4] = acc[4] + E0 * ri + (3.0 * w1 + 2.0 * w2)
    acc[5] = acc[5] + ri - w1
    acc[6] = acc[6] + (w1 - w2)
    acc[7] = acc[7] + w2
    radial = None
    for d in range(3):
        h = (0.5 * DT) * u[d]
        ha = h - 2.0 * DT
        hb = h + 2.0 * DT
        a = [q[k] * ha for k in range(8)]
        b = [q[k] * hb for k in range(8)]
        pu = hp * u[d]
        a[d + 1] = a[d + 1] + hp
        b[d + 1] = b[d + 1] + hp
        a[4] = a[4] + pu
        b[4] = b[4] + pu
        if d == 1:
            radial = (a, b)
        elif d == 0:
            acc = [acc[k] - axial_p(a[k], sub) + axial_m(b[k], sub) for k in range(8)]
        else:
            acc = [acc[k] - lane_p(a[k]) + lane_m(b[k]) for k in range(8)]
    return acc, radial[0], radial[1]


def adjoint_row(q, rate, kind, c, cp, cm, bz, sub, bax):
    r, u, p, inv_t, e1, e2 = primitives(q, rate)
    ri, rs = relax(kind)
    al1 = 3.0 * c[4] - c[5] + c[6]
    al2 = 2.0 * c[4] - c[6] + c[7]
    g1 = e1 * al1
    g2 = e2 * al2
    rate_grad = g1 * q[5]
    gg = (rate_grad + 1.5 * (g2 * q[6])) * inv_t
    ce = (1.0 - 12.0 * DT) - ri
    cmo = ce - rs
    out = [c[k] * (cmo if k in (1, 2, 3) else ce) for k in range(8)]
    out[5] = out[5] + g1
    out[6] = out[6] + g2
    gp = gg * inv_t * r
    rho = -gg * r
    total = [None] * 8
    for d in range(3):
        if d == 0:
            hi = [axial_p(c[k], sub) for k in range(8)]
            lo = [axial_m(c[k], sub) for k in range(8)]
            w = [(hi[k] - lo[k]) + bax * c[k] for k in range(8)]
        elif d == 1:
            hi, lo = cp, cm
            w = [(hi[k] - lo[k]) + bz * c[k] for k in range(8)]
        else:
            hi = [lane_p(c[k]) for k in range(8)]
            lo = [lane_m(c[k]) for k in range(8)]
            w = [hi[k] - lo[k] for k in range(8)]
        total = [hi[k] + lo[k] if total[k] is None else total[k] + (hi[k] + lo[k]) for k in range(8)]
        h = (0.5 * DT) * u[d]
        s = q[0] * w[0]
        for k in range(1, 8):
            s = s + q[k] * w[k]
        s = ((0.5 * DT) * r) * (s + p * w[4])
        out = [out[k] + h * w[k] for k in range(8)]
        out[d + 1] = out[d + 1] + s
        rho = rho - s * u[d]
        gp = gp + ((0.5 * DT) * w[d + 1] + h * w[4])
    gp = GAMMA1 * gp
    rho = rho + (0.5 * gp) * (u[0] * u[0] + u[1] * u[1] + u[2] * u[2])
    out[0] = out[0] + rho
    for j in range(3):
        out[j + 1] = out[j + 1] - gp * u[j]
    out[4] = out[4] + gp
    return [out[k] + (2.0 * DT) * total[k] for k in range(8)], rate_grad


def sub_index():
    return lax.broadcasted_iota(jnp.int32, (1, 8, 128), 1)


def axial_mend():
    t = lax.broadcasted_iota(jnp.int32, (2, 8, 128), 0)
    s = lax.broadcasted_iota(jnp.int32, (2, 8, 128), 1)
    return jnp.where((t == 1) & (s == 7), -2.0, jnp.where((t == 0) & (s == 0), 2.0, 0.0))


def radial_ends():
    pos = lax.axis_index("cross") * lax.axis_size("role") + lax.axis_index("role")
    count = lax.axis_size("cross") * lax.axis_size("role")
    first = R - 2 * pos
    last = R + 2 * (count - pos) - 1
    return first, last


def scalar_mend(j, first, last):
    return jnp.where(j == last, -2.0, jnp.where(j == first, 2.0, 0.0)).astype(F32)


def edge_rows(s):
    lane = iota_lane()
    pack = jnp.where(lane >= 2 * STRIDE, 2, jnp.where(lane >= STRIDE, 1, 0))
    return pack * SLOTS + s


def lane_between(a, b):
    lane = iota_lane()
    return (lane >= a) & (lane < b)


def build_kernel(x_ref, rate_ref, kind_ref, out_ref, pad_ref):
    rows = x_ref.shape[2]
    for f in range(NF):
        v = x_ref[f, 0] if f < 8 else (rate_ref[0] if f == 8 else kind_ref[0].astype(F32))
        pad_ref[f, R : R + rows] = v
        pad_ref[f, 0:R] = jnp.broadcast_to(v[0:1], (R, 128))
        pad_ref[f, R + rows : 2 * R + rows] = jnp.broadcast_to(v[rows - 1 : rows], (R, 128))
    for d in range(out_ref.shape[0]):
        for f in range(NF):
            out_ref[d, f * CHIP : (f + 1) * CHIP] = pad_ref[f, 4 * d : 4 * d + CHIP]


def spread_kernel(own_ref, other_ref, *refs):
    fa_refs, (s0_ref, f_ref, e_ref, fe_ref, left_ref, right_ref) = refs[: RF + 1], refs[RF + 1 :]
    role = lax.axis_index("role")

    def edges(v, j, own, sends):
        p, s = j // SLOTS, j % SLOTS
        base = STRIDE * p
        a = rl(v, base + HALO)
        b = rl(v, base + 3 * HALO - (128 - 2 * HALO))
        w = jnp.where(lane_between(base + HALO, base + 3 * HALO), a, b)
        own[s] = w if own[s] is None else jnp.where(lane_between(base + HALO, base + 5 * HALO), w, own[s])
        k = base + HALO * s
        mk = lane_between(k, k + HALO)
        for i, shift in enumerate((k, k + HALO - 128)):
            t = rl(v, shift)
            sends[i] = t if sends[i] is None else jnp.where(mk, t, sends[i])

    for f in range(NF):
        own, sends = [None] * SLOTS, [None, None]
        for j in range(NROW):
            rows = pl.ds(f * CHIP + j + 2 * role, 8, stride=BLK)
            a, b = own_ref[rows, :], other_ref[rows, :]
            v = jnp.stack([jnp.where(role == 0, a, b), jnp.where(role == 0, b, a)])
            s0_ref[f, j] = v
            edges(v, j, own, sends)
        for s in range(SLOTS):
            e_ref[f, s] = own[s]
        left_ref[f], right_ref[f] = sends
    for f in range(8):
        own, sends = [None] * SLOTS, [None, None]
        for i in range(NFA):
            src = fa_refs[i // 2]
            first = f * 32 + i % 2
            v = jnp.stack([src[pl.ds(first, 8, stride=4), :], src[pl.ds(first + 2, 8, stride=4), :]])
            f_ref[f, i] = v
            edges(v, i + R - RF, own, sends)
        for s in range(SLOTS):
            fe_ref[f, s] = own[s]
        left_ref[NF + f], right_ref[NF + f] = sends


def load(ref, j):
    return [ref[k, j] for k in range(8)]


def store(ref, j, v):
    for k in range(8):
        ref[k, j] = v[k]


def main_kernel(s0_ref, f_ref, out_ref, kg_ref, st_ref, a_ref, b_ref):
    sub, bax = sub_index(), axial_mend()
    first, last = radial_ends()

    def level(src, dst, lo, hi, mix):
        def one(j, _):
            acc, a, b = forward_row(load(src, j), s0_ref[8, j], s0_ref[9, j], sub)
            store(a_ref, j, a)
            store(b_ref, j, b)
            store(dst, j, acc)
            return 0

        def two(j, _):
            jp = jnp.where(j == last, j, j + 1)
            jm = jnp.where(j == first, j, j - 1)
            for k in range(8):
                v = dst[k, j] - a_ref[k, jp] + b_ref[k, jm]
                if mix:
                    v = 0.5 * s0_ref[k, j] + 0.5 * v
                dst[k, j] = v
            return 0

        lax.fori_loop(lo - 1, hi + 2, one, 0)
        lax.fori_loop(lo, hi + 1, two, 0)

    st1, st2, st3 = st_ref.at[0], st_ref.at[1], st_ref.at[2]
    level(s0_ref, st1, 1, NROW - 2, False)
    level(st1, st2, 2, NROW - 3, True)
    level(st2, st3, 3, NROW - 4, False)

    def back(state, c_ref, offset, j):
        jp = jnp.where(j == last, j, j + 1) - offset
        jm = jnp.where(j == first, j, j - 1) - offset
        return adjoint_row(
            load(state, j), s0_ref[8, j], s0_ref[9, j], load(c_ref, j - offset), load(c_ref, jp), load(c_ref, jm),
            scalar_mend(j, first, last), sub, bax,
        )

    foff = R - RF

    def adj3(j, _):
        o, g = back(st3, f_ref, foff, j)
        store(a_ref, j, [0.5 * v for v in o])
        st_ref[2, 0, j] = 0.5 * g
        return 0

    def adj2(j, _):
        o, g = back(st2, a_ref, 0, j)
        store(b_ref, j, [0.5 * f_ref[k, j - foff] + o[k] for k in range(8)])
        st_ref[2, 0, j] = st_ref[2, 0, j] + g
        return 0

    def adj1(j, _):
        o, g = back(st1, b_ref, 0, j)
        store(a_ref, j, [0.5 * v for v in o])
        st_ref[2, 0, j] = st_ref[2, 0, j] + 0.5 * g
        return 0

    def adj0(j, _):
        o, g = back(s0_ref, a_ref, 0, j)
        for k in range(8):
            out_ref[k, j - R] = 0.5 * b_ref[k, j] + o[k]
        kg_ref[j - R] = st_ref[2, 0, j] + g
        return 0

    lax.fori_loop(3, NROW - 3, adj3, 0)
    lax.fori_loop(4, NROW - 4, adj2, 0)
    lax.fori_loop(5, NROW - 5, adj1, 0)
    lax.fori_loop(6, NROW - 6, adj0, 0)


def wrap_slots(ref, k, s, v):
    ref[k, s + 1] = v
    if s == 0:
        ref[k, SLOTS + 1] = rl(v, -STRIDE)
    if s == SLOTS - 1:
        ref[k, 0] = rl(v, STRIDE)


def edge_mend(s, first, last):
    rows = edge_rows(s)
    return rows == first, rows == last


def edge_adjoint(state, e_ref, c_ref, s, first, last, sub, bax):
    mf, ml = edge_mend(s, first, last)
    c = load(c_ref, s + 1)
    cp = [jnp.where(ml, c[k], c_ref[k, s + 2]) for k in range(8)]
    cm = [jnp.where(mf, c[k], c_ref[k, s]) for k in range(8)]
    bz = jnp.where(ml, -2.0, jnp.where(mf, 2.0, 0.0))
    return adjoint_row(load(state, s), e_ref[8, s], e_ref[9, s], c, cp, cm, bz, sub, bax)


def edge_kernel(e_ref, fe_ref, fl_ref, fr_ref, om_ref, kg_ref, out_ref, rg_ref,
                e0_ref, st_ref, a_ref, b_ref, c_ref, fx_ref):
    sub, bax = sub_index(), axial_mend()
    first, last = radial_ends()

    def halo(v, f, s):
        l, r = rl(fl_ref[f], -HALO * s), rl(fr_ref[f], HALO * (5 - s))
        for p in range(3):
            base = STRIDE * p
            v = jnp.where(lane_between(base, base + HALO), l, v)
            v = jnp.where(lane_between(base + 5 * HALO, base + 6 * HALO), r, v)
        return v

    for f in range(NF):
        for s in range(SLOTS):
            e0_ref[f, s] = halo(e_ref[f, s], f, s)
    for f in range(8):
        for s in range(SLOTS):
            wrap_slots(fx_ref, f, s, halo(fe_ref[f, s], NF + f, s))

    def level(src, dst, mix):
        for s in range(SLOTS):
            acc, a, b = forward_row(load(src, s), e0_ref[8, s], e0_ref[9, s], sub)
            store(dst, s, acc)
            for k in range(8):
                wrap_slots(a_ref, k, s, a[k])
                wrap_slots(b_ref, k, s, b[k])
        for s in range(SLOTS):
            mf, ml = edge_mend(s, first, last)
            for k in range(8):
                ap = jnp.where(ml, a_ref[k, s + 1], a_ref[k, s + 2])
                bm = jnp.where(mf, b_ref[k, s + 1], b_ref[k, s])
                v = dst[k, s] - ap + bm
                if mix:
                    v = 0.5 * e0_ref[k, s] + 0.5 * v
                dst[k, s] = v

    st1, st2, st3 = st_ref.at[0], st_ref.at[1], st_ref.at[2]
    level(e0_ref, st1, False)
    level(st1, st2, True)
    level(st2, st3, False)

    def back(state, src, s):
        return edge_adjoint(state, e0_ref, src, s, first, last, sub, bax)

    c3_ref, c2_ref, c1_ref = a_ref, b_ref, c_ref
    grads = [None] * SLOTS
    for s in range(SLOTS):
        o, g = back(st3, fx_ref, s)
        for k in range(8):
            wrap_slots(c3_ref, k, s, 0.5 * o[k])
        grads[s] = 0.5 * g
    for s in range(SLOTS):
        o, g = back(st2, c3_ref, s)
        for k in range(8):
            wrap_slots(c2_ref, k, s, 0.5 * fx_ref[k, s + 1] + o[k])
        grads[s] = grads[s] + g
    for s in range(4):
        o, g = back(st1, c2_ref, s)
        for k in range(8):
            wrap_slots(c1_ref, k, s, 0.5 * o[k])
        grads[s] = grads[s] + 0.5 * g

    head = lane_between(0, HALO)
    tail = lane_between(128 - HALO, 128)

    def merge(m, e):
        return jnp.where(head, rl(e, -(STRIDE + HALO)), jnp.where(tail, rl(e, 128 - HALO - (STRIDE + 4 * HALO)), m))

    for r in range(2):
        s = (R + r) % SLOTS
        o, g = back(e0_ref, c1_ref, s)
        for k in range(8):
            v = merge(om_ref[k, r], 0.5 * c2_ref[k, s + 1] + o[k])
            out_ref[pl.ds(k * 32 + r, 8, stride=4), :] = v[0]
            out_ref[pl.ds(k * 32 + 2 + r, 8, stride=4), :] = v[1]
        v = merge(kg_ref[r], grads[s] + g)
        rg_ref[pl.ds(r, 8, stride=4), :] = v[0]
        rg_ref[pl.ds(2 + r, 8, stride=4), :] = v[1]


def call(kernel, outs, scratch, *args, near=True, leave=False):
    args = [pltpu.with_memory_space_constraint(a, pltpu.VMEM if near else pltpu.HBM) for a in args]
    return pl.pallas_call(
        kernel,
        out_shape=[jax.ShapeDtypeStruct(o, F32) if leave else pltpu.VMEM(o, F32) for o in outs],
        in_specs=[pl.BlockSpec(memory_space=pltpu.VMEM)] * len(args),
        out_specs=[pl.BlockSpec(memory_space=pltpu.VMEM)] * len(outs),
        scratch_shapes=[pltpu.VMEM(s, F32) for s in scratch],
        compiler_params=pltpu.CompilerParams(vmem_limit_bytes=14 * 1024 * 1024),
    )(*args)


T = (2, 8, 128)


def shifted(x, axis, step):
    n = lax.axis_size(axis)
    return lax.ppermute(x, axis, [(i, (i + step) % n) for i in range(n)])


def sections(checkpoint, rate, kinds, final_adjoint):
    chips = lax.axis_size("cross")
    rows = checkpoint.shape[2]
    fa = final_adjoint.reshape(256, 128)
    halo = {}
    for step in (-2, -1, 1, 2):
        halo[step] = shifted(fa, CR, -step)
    (send,) = call(
        build_kernel, [(chips, BLK, 128)], [(NF, rows + 2 * R, 128)], checkpoint, rate, kinds, near=False, leave=True
    )
    own = lax.all_to_all(send, "cross", split_axis=0, concat_axis=0, tiled=True)
    own = own.reshape(chips * BLK, 128)
    other = shifted(own, "role", 1)
    s0, f, e, fe, left, right = call(
        spread_kernel,
        [(NF, NROW) + T, (8, NFA) + T, (NF, SLOTS) + T, (8, SLOTS) + T, (NF + 8,) + T, (NF + 8,) + T],
        [],
        own, other, halo[-2], halo[-1], fa, halo[1], halo[2],
    )
    from_right = shifted(left, "azim", -1)
    from_left = shifted(right, "azim", 1)
    om, kg = call(
        main_kernel,
        [(8, 2) + T, (2,) + T],
        [(3, 8, NROW) + T, (8, NROW) + T, (8, NROW) + T],
        s0, f,
    )
    out, rg = call(
        edge_kernel,
        [(256, 128), (32, 128)],
        [(NF, SLOTS) + T, (3, 8, SLOTS) + T] + [(8, SLOTS + 2) + T] * 4,
        e, fe, from_left, from_right, om, kg, leave=True,
    )
    return out.reshape(8, 16, 2, 128), rg.reshape(16, 2, 128)


def solution(mesh):
    return jax.shard_map(
        sections,
        mesh=mesh,
        in_specs=(
            P(None, CR, None, "azim"),
            P(CR, None, "azim"),
            P(CR, None, "azim"),
            P(None, None, CR, "azim"),
        ),
        out_specs=(P(None, None, CR, "azim"), P(None, CR, "azim")),
        check_vma=False,
    )
```

```python
import jax
import jax.numpy as jnp
from jax import lax
from jax.experimental import pallas as pl
from jax.experimental.pallas import tpu as pltpu
from jax.sharding import PartitionSpec as P


GAMMA1 = 0.3
DT = 0.06
E0 = 1.0 / 0.3 + 0.32

R = 6
RF = 4
NROW = 2 + 2 * R
NFA = 2 + 2 * RF
CHIP = NROW + 2
NF = 10
BLK = NF * CHIP
SLOTS, STRIDE, HALO = 5, 36, 6
CR = ("cross", "role")
F32 = jnp.float32


def iota_lane():
    return lax.broadcasted_iota(jnp.int32, (1, 8, 128), 2)


def rl(x, shift):
    shift %= 128
    return x if shift == 0 else pltpu.roll(x, shift, axis=x.ndim - 1)


def lane_p(x):
    return pltpu.roll(x, 127, axis=2)


def lane_m(x):
    return pltpu.roll(x, 1, axis=2)


def axial_p(x, sub):
    return jnp.concatenate([x[1:], jnp.where(sub == 7, x[1:], pltpu.roll(x[:1], 7, axis=1))], axis=0)


def axial_m(x, sub):
    return jnp.concatenate([jnp.where(sub == 0, x[:1], pltpu.roll(x[1:], 1, axis=1)), x[:1]], axis=0)


def primitives(q, rate):
    r = 1.0 / q[0]
    u = [q[1] * r, q[2] * r, q[3] * r]
    kin = 0.5 * (q[1] * u[0] + q[2] * u[1] + q[3] * u[2])
    p = GAMMA1 * (q[4] - kin)
    inv_t = q[0] / p
    e1 = DT * jnp.exp(rate - inv_t)
    e2 = (2.0 * DT) * jnp.exp(-1.5 * inv_t)
    return r, u, p, inv_t, e1, e2


def relax(kind):
    return jnp.where(kind == 1.0, 2.0 * DT, 0.0), jnp.where(kind == 2.0, DT, 0.0)


def forward_row(q, rate, kind, sub):
    _, u, p, _, e1, e2 = primitives(q, rate)
    ri, rs = relax(kind)
    w1 = e1 * q[5]
    w2 = e2 * q[6]
    hp = (0.5 * DT) * p
    ce = (1.0 - 12.0 * DT) - ri
    cm = ce - rs
    acc = [q[k] * (cm if k in (1, 2, 3) else ce) for k in range(8)]
    acc[0] = acc[0] + ri
    acc[1] = acc[1] + 0.8 * ri
    acc[4] = acc[4] + E0 * ri + (3.0 * w1 + 2.0 * w2)
    acc[5] = acc[5] + ri - w1
    acc[6] = acc[6] + (w1 - w2)
    acc[7] = acc[7] + w2
    radial = None
    for d in range(3):
        h = (0.5 * DT) * u[d]
        ha = h - 2.0 * DT
        hb = h + 2.0 * DT
        a = [q[k] * ha for k in range(8)]
        b = [q[k] * hb for k in range(8)]
        pu = hp * u[d]
        a[d + 1] = a[d + 1] + hp
        b[d + 1] = b[d + 1] + hp
        a[4] = a[4] + pu
        b[4] = b[4] + pu
        if d == 1:
            radial = (a, b)
        elif d == 0:
            acc = [acc[k] - axial_p(a[k], sub) + axial_m(b[k], sub) for k in range(8)]
        else:
            acc = [acc[k] - lane_p(a[k]) + lane_m(b[k]) for k in range(8)]
    return acc, radial[0], radial[1]


def adjoint_row(q, rate, kind, c, cp, cm, bz, sub, bax):
    r, u, p, inv_t, e1, e2 = primitives(q, rate)
    ri, rs = relax(kind)
    al1 = 3.0 * c[4] - c[5] + c[6]
    al2 = 2.0 * c[4] - c[6] + c[7]
    g1 = e1 * al1
    g2 = e2 * al2
    rate_grad = g1 * q[5]
    gg = (rate_grad + 1.5 * (g2 * q[6])) * inv_t
    ce = (1.0 - 12.0 * DT) - ri
    cmo = ce - rs
    out = [c[k] * (cmo if k in (1, 2, 3) else ce) for k in range(8)]
    out[5] = out[5] + g1
    out[6] = out[6] + g2
    gp = gg * inv_t * r
    rho = -gg * r
    total = [None] * 8
    for d in range(3):
        if d == 0:
            hi = [axial_p(c[k], sub) for k in range(8)]
            lo = [axial_m(c[k], sub) for k in range(8)]
            w = [(hi[k] - lo[k]) + bax * c[k] for k in range(8)]
        elif d == 1:
            hi, lo = cp, cm
            w = [(hi[k] - lo[k]) + bz * c[k] for k in range(8)]
        else:
            hi = [lane_p(c[k]) for k in range(8)]
            lo = [lane_m(c[k]) for k in range(8)]
            w = [hi[k] - lo[k] for k in range(8)]
        total = [hi[k] + lo[k] if total[k] is None else total[k] + (hi[k] + lo[k]) for k in range(8)]
        h = (0.5 * DT) * u[d]
        s = q[0] * w[0]
        for k in range(1, 8):
            s = s + q[k] * w[k]
        s = ((0.5 * DT) * r) * (s + p * w[4])
        out = [out[k] + h * w[k] for k in range(8)]
        out[d + 1] = out[d + 1] + s
        rho = rho - s * u[d]
        gp = gp + ((0.5 * DT) * w[d + 1] + h * w[4])
    gp = GAMMA1 * gp
    rho = rho + (0.5 * gp) * (u[0] * u[0] + u[1] * u[1] + u[2] * u[2])
    out[0] = out[0] + rho
    for j in range(3):
        out[j + 1] = out[j + 1] - gp * u[j]
    out[4] = out[4] + gp
    return [out[k] + (2.0 * DT) * total[k] for k in range(8)], rate_grad


def sub_index():
    return lax.broadcasted_iota(jnp.int32, (1, 8, 128), 1)


def axial_mend():
    t = lax.broadcasted_iota(jnp.int32, (2, 8, 128), 0)
    s = lax.broadcasted_iota(jnp.int32, (2, 8, 128), 1)
    return jnp.where((t == 1) & (s == 7), -2.0, jnp.where((t == 0) & (s == 0), 2.0, 0.0))


def radial_ends():
    pos = lax.axis_index("cross") * lax.axis_size("role") + lax.axis_index("role")
    count = lax.axis_size("cross") * lax.axis_size("role")
    first = R - 2 * pos
    last = R + 2 * (count - pos) - 1
    return first, last


def scalar_mend(j, first, last):
    return jnp.where(j == last, -2.0, jnp.where(j == first, 2.0, 0.0)).astype(F32)


def edge_rows(s):
    lane = iota_lane()
    pack = jnp.where(lane >= 2 * STRIDE, 2, jnp.where(lane >= STRIDE, 1, 0))
    return pack * SLOTS + s


def lane_between(a, b):
    lane = iota_lane()
    return (lane >= a) & (lane < b)


def build_kernel(x_ref, rate_ref, kind_ref, out_ref, pad_ref):
    rows = x_ref.shape[2]
    for f in range(NF):
        v = x_ref[f, 0] if f < 8 else (rate_ref[0] if f == 8 else kind_ref[0].astype(F32))
        pad_ref[f, R : R + rows] = v
        pad_ref[f, 0:R] = jnp.broadcast_to(v[0:1], (R, 128))
        pad_ref[f, R + rows : 2 * R + rows] = jnp.broadcast_to(v[rows - 1 : rows], (R, 128))
    for d in range(out_ref.shape[0]):
        for f in range(NF):
            out_ref[d, f * CHIP : (f + 1) * CHIP] = pad_ref[f, 4 * d : 4 * d + CHIP]


def edge_parts(v, j, own, sends):
    p, s = j // SLOTS, j % SLOTS
    base = STRIDE * p
    a = rl(v, base + HALO)
    b = rl(v, base + 3 * HALO - (128 - 2 * HALO))
    w = jnp.where(lane_between(base + HALO, base + 3 * HALO), a, b)
    own[s] = w if own[s] is None else jnp.where(lane_between(base + HALO, base + 5 * HALO), w, own[s])
    k = base + HALO * s
    mk = lane_between(k, k + HALO)
    for i, shift in enumerate((k, k + HALO - 128)):
        t = rl(v, shift)
        sends[i] = t if sends[i] is None else jnp.where(mk, t, sends[i])


def adjoint_spread_kernel(own_ref, mate_ref, near_ref, far_ref, mates_ref, f_ref, fe_ref, left_ref, right_ref):
    is_low = lax.axis_index("role") == 0
    order = ((far_ref, mates_ref), (near_ref, mate_ref), (own_ref, None), (mate_ref, near_ref), (mates_ref, far_ref))

    def pick(i, start):
        low, high = order[i // 2]
        v = low[pl.ds(start, 8, stride=4), :]
        return v if high is None else jnp.where(is_low, v, high[pl.ds(start, 8, stride=4), :])

    for f in range(8):
        own, sends = [None] * SLOTS, [None, None]
        for i in range(NFA):
            first = f * 32 + i % 2
            v = jnp.stack([pick(i, first), pick(i, first + 2)])
            f_ref[f, i] = v
            edge_parts(v, i + R - RF, own, sends)
        for s in range(SLOTS):
            fe_ref[f, s] = own[s]
        left_ref[f], right_ref[f] = sends


def spread_kernel(own_ref, other_ref, fl_ref, fr_ref, s0_ref, e_ref, left_ref, right_ref):
    role = lax.axis_index("role")
    for f in range(NF):
        own, sends = [None] * SLOTS, [None, None]
        for j in range(NROW):
            rows = pl.ds(f * CHIP + j + 2 * role, 8, stride=BLK)
            a, b = own_ref[rows, :], other_ref[rows, :]
            v = jnp.stack([jnp.where(role == 0, a, b), jnp.where(role == 0, b, a)])
            s0_ref[f, j] = v
            edge_parts(v, j, own, sends)
        for s in range(SLOTS):
            e_ref[f, s] = own[s]
        left_ref[f], right_ref[f] = sends
    for f in range(8):
        left_ref[NF + f] = fl_ref[f]
        right_ref[NF + f] = fr_ref[f]


def load(ref, j):
    return [ref[k, j] for k in range(8)]


def store(ref, j, v):
    for k in range(8):
        ref[k, j] = v[k]


def main_kernel(s0_ref, f_ref, out_ref, kg_ref, st_ref, a_ref, b_ref):
    sub, bax = sub_index(), axial_mend()
    first, last = radial_ends()

    def level(src, dst, lo, hi, mix):
        def one(j, _):
            acc, a, b = forward_row(load(src, j), s0_ref[8, j], s0_ref[9, j], sub)
            store(a_ref, j, a)
            store(b_ref, j, b)
            store(dst, j, acc)
            return 0

        def two(j, _):
            jp = jnp.where(j == last, j, j + 1)
            jm = jnp.where(j == first, j, j - 1)
            for k in range(8):
                v = dst[k, j] - a_ref[k, jp] + b_ref[k, jm]
                if mix:
                    v = 0.5 * s0_ref[k, j] + 0.5 * v
                dst[k, j] = v
            return 0

        lax.fori_loop(lo - 1, hi + 2, one, 0)
        lax.fori_loop(lo, hi + 1, two, 0)

    st1, st2, st3 = st_ref.at[0], st_ref.at[1], st_ref.at[2]
    level(s0_ref, st1, 1, NROW - 2, False)
    level(st1, st2, 2, NROW - 3, True)
    level(st2, st3, 3, NROW - 4, False)

    def back(state, c_ref, offset, j):
        jp = jnp.where(j == last, j, j + 1) - offset
        jm = jnp.where(j == first, j, j - 1) - offset
        return adjoint_row(
            load(state, j), s0_ref[8, j], s0_ref[9, j], load(c_ref, j - offset), load(c_ref, jp), load(c_ref, jm),
            scalar_mend(j, first, last), sub, bax,
        )

    foff = R - RF

    def adj3(j, _):
        o, g = back(st3, f_ref, foff, j)
        store(a_ref, j, [0.5 * v for v in o])
        st_ref[2, 0, j] = 0.5 * g
        return 0

    def adj2(j, _):
        o, g = back(st2, a_ref, 0, j)
        store(b_ref, j, [0.5 * f_ref[k, j - foff] + o[k] for k in range(8)])
        st_ref[2, 0, j] = st_ref[2, 0, j] + g
        return 0

    def adj1(j, _):
        o, g = back(st1, b_ref, 0, j)
        store(a_ref, j, [0.5 * v for v in o])
        st_ref[2, 0, j] = st_ref[2, 0, j] + 0.5 * g
        return 0

    def adj0(j, _):
        o, g = back(s0_ref, a_ref, 0, j)
        for k in range(8):
            out_ref[k, j - R] = 0.5 * b_ref[k, j] + o[k]
        kg_ref[j - R] = st_ref[2, 0, j] + g
        return 0

    lax.fori_loop(3, NROW - 3, adj3, 0)
    lax.fori_loop(4, NROW - 4, adj2, 0)
    lax.fori_loop(5, NROW - 5, adj1, 0)
    lax.fori_loop(6, NROW - 6, adj0, 0)


def wrap_slots(ref, k, s, v):
    ref[k, s + 1] = v
    if s == 0:
        ref[k, SLOTS + 1] = rl(v, -STRIDE)
    if s == SLOTS - 1:
        ref[k, 0] = rl(v, STRIDE)


def edge_mend(s, first, last):
    rows = edge_rows(s)
    return rows == first, rows == last


def edge_adjoint(state, e_ref, c_ref, s, first, last, sub, bax):
    mf, ml = edge_mend(s, first, last)
    c = load(c_ref, s + 1)
    cp = [jnp.where(ml, c[k], c_ref[k, s + 2]) for k in range(8)]
    cm = [jnp.where(mf, c[k], c_ref[k, s]) for k in range(8)]
    bz = jnp.where(ml, -2.0, jnp.where(mf, 2.0, 0.0))
    return adjoint_row(load(state, s), e_ref[8, s], e_ref[9, s], c, cp, cm, bz, sub, bax)


def edge_kernel(e_ref, fe_ref, fl_ref, fr_ref, om_ref, kg_ref, out_ref, rg_ref,
                e0_ref, st_ref, a_ref, b_ref, c_ref, fx_ref):
    sub, bax = sub_index(), axial_mend()
    first, last = radial_ends()

    def halo(v, f, s):
        l, r = rl(fl_ref[f], -HALO * s), rl(fr_ref[f], HALO * (5 - s))
        for p in range(3):
            base = STRIDE * p
            v = jnp.where(lane_between(base, base + HALO), l, v)
            v = jnp.where(lane_between(base + 5 * HALO, base + 6 * HALO), r, v)
        return v

    for f in range(NF):
        for s in range(SLOTS):
            e0_ref[f, s] = halo(e_ref[f, s], f, s)
    for f in range(8):
        for s in range(SLOTS):
            wrap_slots(fx_ref, f, s, halo(fe_ref[f, s], NF + f, s))

    def level(src, dst, mix):
        for s in range(SLOTS):
            acc, a, b = forward_row(load(src, s), e0_ref[8, s], e0_ref[9, s], sub)
            store(dst, s, acc)
            for k in range(8):
                wrap_slots(a_ref, k, s, a[k])
                wrap_slots(b_ref, k, s, b[k])
        for s in range(SLOTS):
            mf, ml = edge_mend(s, first, last)
            for k in range(8):
                ap = jnp.where(ml, a_ref[k, s + 1], a_ref[k, s + 2])
                bm = jnp.where(mf, b_ref[k, s + 1], b_ref[k, s])
                v = dst[k, s] - ap + bm
                if mix:
                    v = 0.5 * e0_ref[k, s] + 0.5 * v
                dst[k, s] = v

    st1, st2, st3 = st_ref.at[0], st_ref.at[1], st_ref.at[2]
    level(e0_ref, st1, False)
    level(st1, st2, True)
    level(st2, st3, False)

    def back(state, src, s):
        return edge_adjoint(state, e0_ref, src, s, first, last, sub, bax)

    c3_ref, c2_ref, c1_ref = a_ref, b_ref, c_ref
    grads = [None] * SLOTS
    for s in range(SLOTS):
        o, g = back(st3, fx_ref, s)
        for k in range(8):
            wrap_slots(c3_ref, k, s, 0.5 * o[k])
        grads[s] = 0.5 * g
    for s in range(SLOTS):
        o, g = back(st2, c3_ref, s)
        for k in range(8):
            wrap_slots(c2_ref, k, s, 0.5 * fx_ref[k, s + 1] + o[k])
        grads[s] = grads[s] + g
    for s in range(4):
        o, g = back(st1, c2_ref, s)
        for k in range(8):
            wrap_slots(c1_ref, k, s, 0.5 * o[k])
        grads[s] = grads[s] + 0.5 * g

    head = lane_between(0, HALO)
    tail = lane_between(128 - HALO, 128)

    def merge(m, e):
        return jnp.where(head, rl(e, -(STRIDE + HALO)), jnp.where(tail, rl(e, 128 - HALO - (STRIDE + 4 * HALO)), m))

    for r in range(2):
        s = (R + r) % SLOTS
        o, g = back(e0_ref, c1_ref, s)
        for k in range(8):
            v = merge(om_ref[k, r], 0.5 * c2_ref[k, s + 1] + o[k])
            out_ref[pl.ds(k * 32 + r, 8, stride=4), :] = v[0]
            out_ref[pl.ds(k * 32 + 2 + r, 8, stride=4), :] = v[1]
        v = merge(kg_ref[r], grads[s] + g)
        rg_ref[pl.ds(r, 8, stride=4), :] = v[0]
        rg_ref[pl.ds(2 + r, 8, stride=4), :] = v[1]


def call(kernel, outs, scratch, *args, near=True, leave=False):
    args = [pltpu.with_memory_space_constraint(a, pltpu.VMEM if near else pltpu.HBM) for a in args]
    return pl.pallas_call(
        kernel,
        out_shape=[jax.ShapeDtypeStruct(o, F32) if leave else pltpu.VMEM(o, F32) for o in outs],
        in_specs=[pl.BlockSpec(memory_space=pltpu.VMEM)] * len(args),
        out_specs=[pl.BlockSpec(memory_space=pltpu.VMEM)] * len(outs),
        scratch_shapes=[pltpu.VMEM(s, F32) for s in scratch],
        compiler_params=pltpu.CompilerParams(vmem_limit_bytes=14 * 1024 * 1024),
    )(*args)


T = (2, 8, 128)


def shifted(x, axis, step):
    n = lax.axis_size(axis)
    return lax.ppermute(x, axis, [(i, (i + step) % n) for i in range(n)])


def sections(checkpoint, rate, kinds, final_adjoint):
    chips = lax.axis_size("cross")
    rows = checkpoint.shape[2]
    fa = final_adjoint.reshape(256, 128)
    count = lax.axis_size(CR)
    outward = [(i, (i + (2 if i % 2 == 0 else -2)) % count) for i in range(count)]
    mate = shifted(fa, "role", 1)
    far = lax.ppermute(fa, CR, outward)
    near = lax.ppermute(mate, CR, outward)
    mates = shifted(near, "role", 1)
    (send,) = call(
        build_kernel, [(chips, BLK, 128)], [(NF, rows + 2 * R, 128)], checkpoint, rate, kinds, near=False, leave=True
    )
    own = lax.all_to_all(send, "cross", split_axis=0, concat_axis=0, tiled=True)
    own = own.reshape(chips * BLK, 128)
    other = shifted(own, "role", 1)
    f, fe, fl, fr = call(
        adjoint_spread_kernel,
        [(8, NFA) + T, (8, SLOTS) + T, (8,) + T, (8,) + T],
        [],
        fa, mate, near, far, mates,
    )
    s0, e, left, right = call(
        spread_kernel,
        [(NF, NROW) + T, (NF, SLOTS) + T, (NF + 8,) + T, (NF + 8,) + T],
        [],
        own, other, fl, fr,
    )
    from_right = shifted(left, "azim", -1)
    from_left = shifted(right, "azim", 1)
    om, kg = call(
        main_kernel,
        [(8, 2) + T, (2,) + T],
        [(3, 8, NROW) + T, (8, NROW) + T, (8, NROW) + T],
        s0, f,
    )
    out, rg = call(
        edge_kernel,
        [(256, 128), (32, 128)],
        [(NF, SLOTS) + T, (3, 8, SLOTS) + T] + [(8, SLOTS + 2) + T] * 4,
        e, fe, from_left, from_right, om, kg, leave=True,
    )
    return out.reshape(8, 16, 2, 128), rg.reshape(16, 2, 128)


def solution(mesh):
    return jax.shard_map(
        sections,
        mesh=mesh,
        in_specs=(
            P(None, CR, None, "azim"),
            P(CR, None, "azim"),
            P(CR, None, "azim"),
            P(None, None, CR, "azim"),
        ),
        out_specs=(P(None, None, CR, "azim"), P(None, CR, "azim")),
        check_vma=False,
    )
```

```python
import jax
import jax.numpy as jnp
from jax import lax
from jax.experimental import pallas as pl
from jax.experimental.pallas import tpu as pltpu
from jax.sharding import PartitionSpec as P


GAMMA1 = 0.3
DT = 0.06
E0 = 1.0 / 0.3 + 0.32

R = 6
RF = 4
NROW = 2 + 2 * R
NFA = 2 + 2 * RF
CHIP = NROW + 2
NF = 10
BLK = NF * CHIP
SLOTS, STRIDE, HALO = 5, 36, 6
CR = ("cross", "role")
F32 = jnp.float32


def iota_lane():
    return lax.broadcasted_iota(jnp.int32, (1, 8, 128), 2)


def rl(x, shift):
    shift %= 128
    return x if shift == 0 else pltpu.roll(x, shift, axis=x.ndim - 1)


def lane_p(x):
    return pltpu.roll(x, 127, axis=2)


def lane_m(x):
    return pltpu.roll(x, 1, axis=2)


def axial_p(x, sub):
    return jnp.concatenate([x[1:], jnp.where(sub == 7, x[1:], pltpu.roll(x[:1], 7, axis=1))], axis=0)


def axial_m(x, sub):
    return jnp.concatenate([jnp.where(sub == 0, x[:1], pltpu.roll(x[1:], 1, axis=1)), x[:1]], axis=0)


def primitives(q, rate):
    r = 1.0 / q[0]
    u = [q[1] * r, q[2] * r, q[3] * r]
    kin = 0.5 * (q[1] * u[0] + q[2] * u[1] + q[3] * u[2])
    p = GAMMA1 * (q[4] - kin)
    inv_t = q[0] / p
    e1 = DT * jnp.exp(rate - inv_t)
    e2 = (2.0 * DT) * jnp.exp(-1.5 * inv_t)
    return [r, *u, p, inv_t, e1, e2]


def relax(kind):
    return jnp.where(kind == 1.0, 2.0 * DT, 0.0), jnp.where(kind == 2.0, DT, 0.0)


def forward_row(q, rate, kind, sub):
    prim = primitives(q, rate)
    u, (p, inv_t, e1, e2) = prim[1:4], prim[4:]
    ri, rs = relax(kind)
    w1 = e1 * q[5]
    w2 = e2 * q[6]
    hp = (0.5 * DT) * p
    ce = (1.0 - 12.0 * DT) - ri
    cm = ce - rs
    acc = [q[k] * (cm if k in (1, 2, 3) else ce) for k in range(8)]
    acc[0] = acc[0] + ri
    acc[1] = acc[1] + 0.8 * ri
    acc[4] = acc[4] + E0 * ri + (3.0 * w1 + 2.0 * w2)
    acc[5] = acc[5] + ri - w1
    acc[6] = acc[6] + (w1 - w2)
    acc[7] = acc[7] + w2
    radial = None
    for d in range(3):
        h = (0.5 * DT) * u[d]
        ha = h - 2.0 * DT
        hb = h + 2.0 * DT
        a = [q[k] * ha for k in range(8)]
        b = [q[k] * hb for k in range(8)]
        pu = hp * u[d]
        a[d + 1] = a[d + 1] + hp
        b[d + 1] = b[d + 1] + hp
        a[4] = a[4] + pu
        b[4] = b[4] + pu
        if d == 1:
            radial = (a, b)
        elif d == 0:
            acc = [acc[k] - axial_p(a[k], sub) + axial_m(b[k], sub) for k in range(8)]
        else:
            acc = [acc[k] - lane_p(a[k]) + lane_m(b[k]) for k in range(8)]
    return acc, radial[0], radial[1], prim


def radial_share(q, sign):
    r = 1.0 / q[0]
    u = q[2] * r
    p = GAMMA1 * (q[4] - (0.5 * r) * (q[1] * q[1] + q[2] * q[2] + q[3] * q[3]))
    hp = (0.5 * DT) * p
    h = (0.5 * DT) * u + sign * 2.0 * DT
    share = [q[k] * h for k in range(8)]
    share[2] = share[2] + hp
    share[4] = share[4] + hp * u
    return share


def adjoint_row(q, prim, kind, c, cp, cm, bz, sub, bax):
    r, u, (p, inv_t, e1, e2) = prim[0], prim[1:4], prim[4:]
    ri, rs = relax(kind)
    al1 = 3.0 * c[4] - c[5] + c[6]
    al2 = 2.0 * c[4] - c[6] + c[7]
    g1 = e1 * al1
    g2 = e2 * al2
    rate_grad = g1 * q[5]
    gg = (rate_grad + 1.5 * (g2 * q[6])) * inv_t
    ce = (1.0 - 12.0 * DT) - ri
    cmo = ce - rs
    out = [c[k] * (cmo if k in (1, 2, 3) else ce) for k in range(8)]
    out[5] = out[5] + g1
    out[6] = out[6] + g2
    gp = gg * inv_t * r
    rho = -gg * r
    total = [None] * 8
    for d in range(3):
        if d == 0:
            hi = [axial_p(c[k], sub) for k in range(8)]
            lo = [axial_m(c[k], sub) for k in range(8)]
            w = [(hi[k] - lo[k]) + bax * c[k] for k in range(8)]
        elif d == 1:
            hi, lo = cp, cm
            w = [(hi[k] - lo[k]) + bz * c[k] for k in range(8)]
        else:
            hi = [lane_p(c[k]) for k in range(8)]
            lo = [lane_m(c[k]) for k in range(8)]
            w = [hi[k] - lo[k] for k in range(8)]
        total = [hi[k] + lo[k] if total[k] is None else total[k] + (hi[k] + lo[k]) for k in range(8)]
        h = (0.5 * DT) * u[d]
        s = q[0] * w[0]
        for k in range(1, 8):
            s = s + q[k] * w[k]
        s = ((0.5 * DT) * r) * (s + p * w[4])
        out = [out[k] + h * w[k] for k in range(8)]
        out[d + 1] = out[d + 1] + s
        rho = rho - s * u[d]
        gp = gp + ((0.5 * DT) * w[d + 1] + h * w[4])
    gp = GAMMA1 * gp
    rho = rho + (0.5 * gp) * (u[0] * u[0] + u[1] * u[1] + u[2] * u[2])
    out[0] = out[0] + rho
    for j in range(3):
        out[j + 1] = out[j + 1] - gp * u[j]
    out[4] = out[4] + gp
    return [out[k] + (2.0 * DT) * total[k] for k in range(8)], rate_grad


def sub_index():
    return lax.broadcasted_iota(jnp.int32, (1, 8, 128), 1)


def axial_mend():
    t = lax.broadcasted_iota(jnp.int32, (2, 8, 128), 0)
    s = lax.broadcasted_iota(jnp.int32, (2, 8, 128), 1)
    return jnp.where((t == 1) & (s == 7), -2.0, jnp.where((t == 0) & (s == 0), 2.0, 0.0))


def radial_ends():
    pos = lax.axis_index("cross") * lax.axis_size("role") + lax.axis_index("role")
    count = lax.axis_size("cross") * lax.axis_size("role")
    first = R - 2 * pos
    last = R + 2 * (count - pos) - 1
    return first, last


def scalar_mend(j, first, last):
    return jnp.where(j == last, -2.0, jnp.where(j == first, 2.0, 0.0)).astype(F32)


def edge_rows(s):
    lane = iota_lane()
    pack = jnp.where(lane >= 2 * STRIDE, 2, jnp.where(lane >= STRIDE, 1, 0))
    return pack * SLOTS + s


def lane_between(a, b):
    lane = iota_lane()
    return (lane >= a) & (lane < b)


def build_kernel(x_ref, rate_ref, kind_ref, out_ref, pad_ref):
    rows = x_ref.shape[2]
    for f in range(NF):
        v = x_ref[f, 0] if f < 8 else (rate_ref[0] if f == 8 else kind_ref[0].astype(F32))
        pad_ref[f, R : R + rows] = v
        pad_ref[f, 0:R] = jnp.broadcast_to(v[0:1], (R, 128))
        pad_ref[f, R + rows : 2 * R + rows] = jnp.broadcast_to(v[rows - 1 : rows], (R, 128))
    for d in range(out_ref.shape[0]):
        for f in range(NF):
            out_ref[d, f * CHIP : (f + 1) * CHIP] = pad_ref[f, 4 * d : 4 * d + CHIP]


def edge_parts(v, j, own, sends):
    p, s = j // SLOTS, j % SLOTS
    base = STRIDE * p
    a = rl(v, base + HALO)
    b = rl(v, base + 3 * HALO - (128 - 2 * HALO))
    w = jnp.where(lane_between(base + HALO, base + 3 * HALO), a, b)
    own[s] = w if own[s] is None else jnp.where(lane_between(base + HALO, base + 5 * HALO), w, own[s])
    k = base + HALO * s
    mk = lane_between(k, k + HALO)
    for i, shift in enumerate((k, k + HALO - 128)):
        t = rl(v, shift)
        sends[i] = t if sends[i] is None else jnp.where(mk, t, sends[i])


def adjoint_spread_kernel(own_ref, mate_ref, near_ref, far_ref, mates_ref, f_ref, fe_ref, left_ref, right_ref):
    is_low = lax.axis_index("role") == 0
    order = ((far_ref, mates_ref), (near_ref, mate_ref), (own_ref, None), (mate_ref, near_ref), (mates_ref, far_ref))

    def pick(i, start):
        low, high = order[i // 2]
        v = low[pl.ds(start, 8, stride=4), :]
        return v if high is None else jnp.where(is_low, v, high[pl.ds(start, 8, stride=4), :])

    for f in range(8):
        own, sends = [None] * SLOTS, [None, None]
        for i in range(NFA):
            first = f * 32 + i % 2
            v = jnp.stack([pick(i, first), pick(i, first + 2)])
            f_ref[f, i] = v
            edge_parts(v, i + R - RF, own, sends)
        for s in range(SLOTS):
            fe_ref[f, s] = own[s]
        left_ref[f], right_ref[f] = sends


def spread_kernel(own_ref, other_ref, fl_ref, fr_ref, s0_ref, e_ref, left_ref, right_ref):
    role = lax.axis_index("role")
    for f in range(NF):
        own, sends = [None] * SLOTS, [None, None]
        for j in range(NROW):
            rows = pl.ds(f * CHIP + j + 2 * role, 8, stride=BLK)
            a, b = own_ref[rows, :], other_ref[rows, :]
            v = jnp.stack([jnp.where(role == 0, a, b), jnp.where(role == 0, b, a)])
            s0_ref[f, j] = v
            edge_parts(v, j, own, sends)
        for s in range(SLOTS):
            e_ref[f, s] = own[s]
        left_ref[f], right_ref[f] = sends
    for f in range(8):
        left_ref[NF + f] = fl_ref[f]
        right_ref[NF + f] = fr_ref[f]


def load(ref, j):
    return [ref[k, j] for k in range(8)]


def store(ref, j, v):
    for k in range(8):
        ref[k, j] = v[k]


def main_kernel(s0_ref, f_ref, out_ref, kg_ref, st_ref, a_refs, b_refs, pr_ref, g_ref):
    sub, bax = sub_index(), axial_mend()
    first, last = radial_ends()
    n = NROW

    def above(j):
        return jnp.where(j == last, j, j + 1)

    def below(j):
        return jnp.where(j == first, j, j - 1)

    def state(level, j):
        acc, a_ref, b_ref = st_ref.at[level - 1], a_refs.at[(level - 1) % 2], b_refs.at[(level - 1) % 2]
        v = [acc[k, j] - a_ref[k, above(j)] + b_ref[k, below(j)] for k in range(8)]
        return [0.5 * s0_ref[k, j] + 0.5 * v[k] for k in range(8)] if level == 2 else v

    def advance(level):
        get = (lambda j: load(s0_ref, j)) if level == 0 else (lambda j: state(level, j))
        a_ref, b_ref = a_refs.at[level % 2], b_refs.at[level % 2]
        store(b_ref, level, radial_share(get(level), 1.0))
        store(a_ref, n - 1 - level, radial_share(get(n - 1 - level), -1.0))

        def one(j, _):
            q = get(j)
            if level > 0:
                store(st_ref.at[level - 1], j, q)
            acc, a, b, prim = forward_row(q, s0_ref[8, j], s0_ref[9, j], sub)
            store(a_ref, j, a)
            store(b_ref, j, b)
            store(st_ref.at[level], j, acc)
            store(pr_ref.at[level], j, prim)
            return 0

        lax.fori_loop(level + 1, n - 1 - level, one, 0, unroll=(4, 5, 4)[level])

    for level in range(3):
        advance(level)

    def back(q, prim, c_ref, offset, j):
        jp, jm = above(j) - offset, below(j) - offset
        return adjoint_row(
            q, prim, s0_ref[9, j], load(c_ref, j - offset), load(c_ref, jp), load(c_ref, jm),
            scalar_mend(j, first, last), sub, bax,
        )

    foff = R - RF
    c3_ref, c2_ref, c1_ref = a_refs.at[1], b_refs.at[1], a_refs.at[0]

    def adj3(j, _):
        q = state(3, j)
        o, g = back(q, primitives(q, s0_ref[8, j]), f_ref, foff, j)
        store(c3_ref, j, [0.5 * v for v in o])
        g_ref[j] = 0.5 * g
        return 0

    def adj2(j, _):
        o, g = back(load(st_ref.at[1], j), load(pr_ref.at[2], j), c3_ref, 0, j)
        store(c2_ref, j, [0.5 * f_ref[k, j - foff] + o[k] for k in range(8)])
        g_ref[j] = g_ref[j] + g
        return 0

    def adj1(j, _):
        o, g = back(load(st_ref.at[0], j), load(pr_ref.at[1], j), c2_ref, 0, j)
        store(c1_ref, j, [0.5 * v for v in o])
        g_ref[j] = g_ref[j] + 0.5 * g
        return 0

    def adj0(j, _):
        o, g = back(load(s0_ref, j), load(pr_ref.at[0], j), c1_ref, 0, j)
        for k in range(8):
            out_ref[k, j - R] = 0.5 * c2_ref[k, j] + o[k]
        kg_ref[j - R] = g_ref[j] + g
        return 0

    for i, body in enumerate((adj3, adj2, adj1, adj0)):
        lax.fori_loop(3 + i, n - 3 - i, body, 0, unroll=(4, 3, 4, 2)[i])


def wrap_slots(ref, k, s, v):
    ref[k, s + 1] = v
    if s == 0:
        ref[k, SLOTS + 1] = rl(v, -STRIDE)
    if s == SLOTS - 1:
        ref[k, 0] = rl(v, STRIDE)


def edge_mend(s, first, last):
    rows = edge_rows(s)
    return rows == first, rows == last


def edge_adjoint(q, prim, kind, c_ref, s, first, last, sub, bax):
    mf, ml = edge_mend(s, first, last)
    c = load(c_ref, s + 1)
    cp = [jnp.where(ml, c[k], c_ref[k, s + 2]) for k in range(8)]
    cm = [jnp.where(mf, c[k], c_ref[k, s]) for k in range(8)]
    bz = jnp.where(ml, -2.0, jnp.where(mf, 2.0, 0.0))
    return adjoint_row(q, prim, kind, c, cp, cm, bz, sub, bax)


def edge_kernel(e_ref, fe_ref, fl_ref, fr_ref, om_ref, kg_ref, out_ref, rg_ref,
                e0_ref, st_ref, a_ref, b_ref, c_ref, fx_ref, pr_ref):
    sub, bax = sub_index(), axial_mend()
    first, last = radial_ends()

    def halo(v, f, s):
        l, r = rl(fl_ref[f], -HALO * s), rl(fr_ref[f], HALO * (5 - s))
        for p in range(3):
            base = STRIDE * p
            v = jnp.where(lane_between(base, base + HALO), l, v)
            v = jnp.where(lane_between(base + 5 * HALO, base + 6 * HALO), r, v)
        return v

    for f in range(NF):
        for s in range(SLOTS):
            e0_ref[f, s] = halo(e_ref[f, s], f, s)
    for f in range(8):
        for s in range(SLOTS):
            wrap_slots(fx_ref, f, s, halo(fe_ref[f, s], NF + f, s))

    def level(src, dst, i, mix):
        for s in range(SLOTS):
            acc, a, b, prim = forward_row(load(src, s), e0_ref[8, s], e0_ref[9, s], sub)
            store(dst, s, acc)
            store(pr_ref.at[i], s, prim)
            for k in range(8):
                wrap_slots(a_ref, k, s, a[k])
                wrap_slots(b_ref, k, s, b[k])
        for s in range(SLOTS):
            mf, ml = edge_mend(s, first, last)
            for k in range(8):
                ap = jnp.where(ml, a_ref[k, s + 1], a_ref[k, s + 2])
                bm = jnp.where(mf, b_ref[k, s + 1], b_ref[k, s])
                v = dst[k, s] - ap + bm
                if mix:
                    v = 0.5 * e0_ref[k, s] + 0.5 * v
                dst[k, s] = v

    st1, st2, st3 = st_ref.at[0], st_ref.at[1], st_ref.at[2]
    level(e0_ref, st1, 0, False)
    level(st1, st2, 1, True)
    level(st2, st3, 2, False)

    def back(state, i, src, s):
        q = load(state, s)
        prim = primitives(q, e0_ref[8, s]) if i == 3 else load(pr_ref.at[i], s)
        return edge_adjoint(q, prim, e0_ref[9, s], src, s, first, last, sub, bax)

    c3_ref, c2_ref, c1_ref = a_ref, b_ref, c_ref
    grads = [None] * SLOTS
    for s in range(SLOTS):
        o, g = back(st3, 3, fx_ref, s)
        for k in range(8):
            wrap_slots(c3_ref, k, s, 0.5 * o[k])
        grads[s] = 0.5 * g
    for s in range(SLOTS):
        o, g = back(st2, 2, c3_ref, s)
        for k in range(8):
            wrap_slots(c2_ref, k, s, 0.5 * fx_ref[k, s + 1] + o[k])
        grads[s] = grads[s] + g
    for s in range(4):
        o, g = back(st1, 1, c2_ref, s)
        for k in range(8):
            wrap_slots(c1_ref, k, s, 0.5 * o[k])
        grads[s] = grads[s] + 0.5 * g

    head = lane_between(0, HALO)
    tail = lane_between(128 - HALO, 128)

    def merge(m, e):
        return jnp.where(head, rl(e, -(STRIDE + HALO)), jnp.where(tail, rl(e, 128 - HALO - (STRIDE + 4 * HALO)), m))

    for r in range(2):
        s = (R + r) % SLOTS
        o, g = back(e0_ref, 0, c1_ref, s)
        for k in range(8):
            v = merge(om_ref[k, r], 0.5 * c2_ref[k, s + 1] + o[k])
            out_ref[pl.ds(k * 32 + r, 8, stride=4), :] = v[0]
            out_ref[pl.ds(k * 32 + 2 + r, 8, stride=4), :] = v[1]
        v = merge(kg_ref[r], grads[s] + g)
        rg_ref[pl.ds(r, 8, stride=4), :] = v[0]
        rg_ref[pl.ds(2 + r, 8, stride=4), :] = v[1]


def call(kernel, outs, scratch, *args, near=True, leave=False):
    args = [pltpu.with_memory_space_constraint(a, pltpu.VMEM if near else pltpu.HBM) for a in args]
    return pl.pallas_call(
        kernel,
        out_shape=[jax.ShapeDtypeStruct(o, F32) if leave else pltpu.VMEM(o, F32) for o in outs],
        in_specs=[pl.BlockSpec(memory_space=pltpu.VMEM)] * len(args),
        out_specs=[pl.BlockSpec(memory_space=pltpu.VMEM)] * len(outs),
        scratch_shapes=[pltpu.VMEM(s, F32) for s in scratch],
        compiler_params=pltpu.CompilerParams(vmem_limit_bytes=18 * 1024 * 1024),
    )(*args)


T = (2, 8, 128)


def shifted(x, axis, step):
    n = lax.axis_size(axis)
    return lax.ppermute(x, axis, [(i, (i + step) % n) for i in range(n)])


def sections(checkpoint, rate, kinds, final_adjoint):
    chips = lax.axis_size("cross")
    rows = checkpoint.shape[2]
    fa = final_adjoint.reshape(256, 128)
    count = lax.axis_size(CR)
    outward = [(i, (i + (2 if i % 2 == 0 else -2)) % count) for i in range(count)]
    mate = shifted(fa, "role", 1)
    far = lax.ppermute(fa, CR, outward)
    near = lax.ppermute(mate, CR, outward)
    mates = shifted(near, "role", 1)
    (send,) = call(
        build_kernel, [(chips, BLK, 128)], [(NF, rows + 2 * R, 128)], checkpoint, rate, kinds, near=False, leave=True
    )
    own = lax.all_to_all(send, "cross", split_axis=0, concat_axis=0, tiled=True)
    own = own.reshape(chips * BLK, 128)
    other = shifted(own, "role", 1)
    f, fe, fl, fr = call(
        adjoint_spread_kernel,
        [(8, NFA) + T, (8, SLOTS) + T, (8,) + T, (8,) + T],
        [],
        fa, mate, near, far, mates,
    )
    s0, e, left, right = call(
        spread_kernel,
        [(NF, NROW) + T, (NF, SLOTS) + T, (NF + 8,) + T, (NF + 8,) + T],
        [],
        own, other, fl, fr,
    )
    from_right = shifted(left, "azim", -1)
    from_left = shifted(right, "azim", 1)
    om, kg = call(
        main_kernel,
        [(8, 2) + T, (2,) + T],
        [(3, 8, NROW) + T, (2, 8, NROW) + T, (2, 8, NROW) + T, (3, 8, NROW) + T, (NROW,) + T],
        s0, f,
    )
    out, rg = call(
        edge_kernel,
        [(256, 128), (32, 128)],
        [(NF, SLOTS) + T, (3, 8, SLOTS) + T] + [(8, SLOTS + 2) + T] * 4 + [(3, 8, SLOTS) + T],
        e, fe, from_left, from_right, om, kg, leave=True,
    )
    return out.reshape(8, 16, 2, 128), rg.reshape(16, 2, 128)


def solution(mesh):
    return jax.shard_map(
        sections,
        mesh=mesh,
        in_specs=(
            P(None, CR, None, "azim"),
            P(CR, None, "azim"),
            P(CR, None, "azim"),
            P(None, None, CR, "azim"),
        ),
        out_specs=(P(None, None, CR, "azim"), P(None, CR, "azim")),
        check_vma=False,
    )
```
